32 devices in a mesh: group: 2 (over x), engine: 4 (over y, core), chan: 4 (over z).
Axes of the slice: x: 2, y: 2, z: 4, core: 2. Of those that a mesh axis runs over, the one named last changes fastest.
Arguments:
- mr_qkv: bfloat16 [2, 3, 128, 8192], P(None, None, ('group', 'engine'), 'chan'), parts along dimension 2, may hold values from -6 to 6
- li_qkv: bfloat16 [2, 3, 128, 8192], P(None, None, ('group', 'engine'), 'chan'), parts along dimension 2, may hold values from -6 to 6
- conv_tails: bfloat16 [128, 127, 8192], P(('group', 'engine'), None, 'chan'), parts along dimension 0, may hold values from -6 to 6
- modal_states: float32 [128, 16, 8192], P(('group', 'engine'), None, 'chan'), parts along dimension 0, may hold values from -12 to 12
- source: int32 [128], P('group'), parts along dimension 0, may hold values from 0 to 63, as said below
- remaining: int32 [128], P(('group', 'engine')), parts along dimension 0, may hold values from 0 to 3
- mr_filter: bfloat16 [128, 8192], P(None, 'chan'), may hold values from -0.5 to 0.5
- li_decay: float32 [16, 8192], P(None, 'chan'), may hold values from 0.5 to 0.999
- li_residue: float32 [16, 8192], P(None, 'chan'), may hold values from -1.5 to 1.5
- mr_panels: bfloat16 [8, 8192, 512], P('engine', 'chan'), may hold values from -0.046875 to 0.046875
- li_panels: bfloat16 [8, 8192, 512], P('engine', 'chan'), may hold values from -0.046875 to 0.046875
- panel_slot: int32 [8], replicated, may hold values from 0 to 7, each once
Outputs:
- mixed: bfloat16 [2, 128, 4096], P(None, ('group', 'engine'), 'chan'), parts along dimension 1
- new_tails: bfloat16 [128, 127, 8192], P(('group', 'engine'), None, 'chan'), parts along dimension 0
- new_states: float32 [128, 16, 8192], P(('group', 'engine'), None, 'chan'), parts along dimension 0
The draws below stay inside these ranges and needn't reach their ends.
There are 2 independent parts, one for each index of `group`. The reference program is written for one: setup_inputs(seed, part) draws one part's arguments, and reference() takes and returns one part's arrays. A program takes and returns all parts, laid end to end along the dimension named above; an argument that names none is the same for every part. Nothing has to cross between parts.
Inputs may be any that keep to these rules, and one draw needn't show every extreme that they name: `source`: A permutation of the old slots. Each engine's 16 new slots hold exactly 2 rollouts from each of 3 other engines and 10 rollouts from its own old slots; engine e takes from the engines e - d mod 4 for 3 distances d that are the same for every engine, so every engine also gives exactly 2 rollouts to each of 3 others.
All inputs are finite; a program needn't handle non-finite values.
Results may differ from the reference program's by a relative error of at most 0.008.
Values may be sent and summed in bfloat16 or wider, within the bound.
No kernel may reach another device: no remote copies, remote signals or barrier semaphores. Data moves between devices by JAX's collectives and lax.ppermute only.
A program may use at most 192 MiB of HBM per device.

```python
import math
import jax
import jax.numpy as jnp
from jax import lax

D = 8192
OUTW = 4096
TAPS = 128
STATE = 16
R_DEV = 16
CAP = 2
TAIL = 127
NB = 3
ROLL = 64
PANELS = 8
PW = 512
N_ENGINE = 4


def draw_source(key, part):
    key_shift = jax.random.fold_in(key, 11)
    key_old = jax.random.fold_in(key, 12)
    key_new = jax.random.fold_in(key, 13)
    shifts = jax.random.permutation(key_shift, N_ENGINE - 1) + 1
    keep_count = R_DEV - CAP * NB
    old_perm = jax.vmap(lambda k: jax.random.permutation(k, R_DEV))(jax.random.split(key_old, N_ENGINE))
    new_perm = jax.vmap(lambda k: jax.random.permutation(k, R_DEV))(jax.random.split(key_new, N_ENGINE))
    dest = jnp.broadcast_to(jnp.arange(N_ENGINE)[:, None], (N_ENGINE, R_DEV))
    place = jnp.broadcast_to(jnp.arange(R_DEV)[None, :], (N_ENGINE, R_DEV))
    batch = jnp.clip((place - keep_count) // CAP, 0, NB - 1)
    src_engine = jnp.where(place < keep_count, dest, (dest - shifts[batch]) % N_ENGINE)
    local = old_perm[src_engine, place]
    old_slot = (src_engine * R_DEV + local).astype(jnp.int32)
    new_slot = (dest * R_DEV + new_perm).astype(jnp.int32)
    return jnp.zeros((ROLL,), jnp.int32).at[new_slot.reshape(-1)].set(old_slot.reshape(-1))


def place_ends(array, own_key, low, largest):
    shape = array.shape
    spot = [jax.random.randint(jax.random.fold_in(own_key, axis), (), 0, shape[axis]) for axis in range(len(shape))]
    array = array.at[tuple(spot)].set(low)
    longest = shape.index(max(shape))
    spot[longest] = (spot[longest] + 1) % shape[longest]
    return array.at[tuple(spot)].set(largest)


def steps_of(rng, shape, pieces, least, largest):
    level = 1.0
    for position, blocks in pieces:
        draws = jax.random.uniform(jax.random.fold_in(jax.random.fold_in(rng, 6), position), (blocks,), jnp.float32, least / len(pieces), largest / len(pieces))
        level = level * jnp.repeat(jnp.exp(draws), shape[position] // blocks).reshape((-1,) + (1,) * (len(shape) - 1 - position))
    return level


def gaussian(own_key, extent, deviation, reach, pieces=(), kind=jnp.bfloat16):
    entries = deviation * jax.random.normal(own_key, extent, jnp.float32)
    if pieces:
        entries = entries * steps_of(own_key, extent, pieces, -0.22, 0.18)
    return jnp.clip(entries, -reach, reach).astype(kind)


def setup_inputs(seed: int = 0, part: int = 0) -> dict:
    streams_of = jax.random.split(jax.random.key(seed), 13)
    part_splits = jax.random.split(jax.random.fold_in(streams_of[12], part), 13)
    mr_qkv = gaussian(part_splits[0], (2, 3, ROLL, D), 1.0, 6.0, ((2, 4), (3, 4)))
    li_qkv = gaussian(part_splits[1], (2, 3, ROLL, D), 1.0, 6.0, ((2, 4), (3, 4)))
    conv_tails = gaussian(part_splits[2], (ROLL, TAIL, D), 1.0, 6.0, ((0, 4), (2, 4)))
    modal_states = gaussian(part_splits[3], (ROLL, STATE, D), 2.0, 12.0, ((0, 4), (2, 4)), jnp.float32)
    source = draw_source(jax.random.fold_in(jax.random.fold_in(streams_of[12], part), 71), part)
    remaining = place_ends(jax.random.randint(part_splits[5], (ROLL,), 0, 4), jax.random.fold_in(part_splits[5], 1), 0, 3).astype(jnp.int32)
    mr_filter = gaussian(streams_of[6], (TAPS, D), TAPS ** -0.5, 0.5, ((1, 4),))
    li_decay = jnp.clip(jnp.exp(math.log(0.999) - 0.6921467 * jax.random.uniform(streams_of[7], (STATE, D), jnp.float32) ** steps_of(streams_of[7], (STATE, D), ((1, 4),), -0.2, 0.2)), 0.5, 0.999)
    li_residue = gaussian(streams_of[8], (STATE, D), STATE ** -0.5, 1.5, ((1, 4),), jnp.float32)
    mr_panels = gaussian(streams_of[9], (PANELS, D, PW), (2 * D) ** -0.5, 0.046875, ((0, 4), (1, 4)))
    li_panels = gaussian(streams_of[10], (PANELS, D, PW), (2 * D) ** -0.5, 0.046875, ((0, 4), (1, 4)))
    panel_slot = jax.random.permutation(streams_of[11], PANELS).astype(jnp.int32)
    return dict(mr_qkv=mr_qkv, li_qkv=li_qkv, conv_tails=conv_tails, modal_states=modal_states, source=source, remaining=remaining, mr_filter=mr_filter, li_decay=li_decay, li_residue=li_residue, mr_panels=mr_panels, li_panels=li_panels, panel_slot=panel_slot)


def full_matrix(panels, panel_slot):
    chosen = panels[panel_slot]
    return jnp.transpose(chosen, (1, 0, 2)).reshape(D, OUTW)


def reference(mr_qkv, li_qkv, conv_tails, modal_states, source, remaining, mr_filter, li_decay, li_residue, mr_panels, li_panels, panel_slot):
    filt = mr_filter.astype(jnp.float32)
    zmr_first = (mr_qkv[0, 1].astype(jnp.float32) * mr_qkv[0, 2].astype(jnp.float32)).astype(jnp.bfloat16)
    zmr_second = (mr_qkv[1, 1].astype(jnp.float32) * mr_qkv[1, 2].astype(jnp.float32)).astype(jnp.bfloat16)
    blocks = source.reshape(N_ENGINE, R_DEV)
    first_blocks = zmr_first.reshape(N_ENGINE, R_DEV, D)
    second_blocks = zmr_second.reshape(N_ENGINE, R_DEV, D)

    def conv_block(inputs):
        index_rows, first_z, second_z = inputs
        tail_blk = conv_tails[index_rows]
        tail_f = tail_blk.astype(jnp.float32)
        first = jnp.einsum("rtc,tc->rc", tail_f, filt[1:])
        second = jnp.einsum("rtc,tc->rc", tail_f[:, :TAIL - 1], filt[2:])
        advanced = jnp.concatenate([second_z[:, None, :], first_z[:, None, :], tail_blk[:, :TAIL - 2]], axis=1)
        return jnp.stack([first, second]), advanced

    parts, advanced = lax.map(conv_block, (blocks, first_blocks, second_blocks))
    parts = jnp.transpose(parts, (1, 0, 2, 3)).reshape(2, ROLL, D)
    new_tails = advanced.reshape(ROLL, TAIL, D)
    zmr0 = zmr_first.astype(jnp.float32)
    zmr1 = zmr_second.astype(jnp.float32)
    conv0 = filt[0] * zmr0 + parts[0]
    conv1 = filt[0] * zmr1 + filt[1] * zmr0 + parts[1]
    ymr0 = (mr_qkv[0, 0].astype(jnp.float32) * conv0).astype(jnp.bfloat16)
    ymr1 = (mr_qkv[1, 0].astype(jnp.float32) * conv1).astype(jnp.bfloat16)
    states = modal_states[source]
    zli0 = (li_qkv[0, 1].astype(jnp.float32) * li_qkv[0, 2].astype(jnp.float32)).astype(jnp.bfloat16).astype(jnp.float32)
    zli1 = (li_qkv[1, 1].astype(jnp.float32) * li_qkv[1, 2].astype(jnp.float32)).astype(jnp.bfloat16).astype(jnp.float32)
    states1 = li_decay[None] * states + zli0[:, None, :]
    yli0 = (li_qkv[0, 0].astype(jnp.float32) * jnp.sum(li_residue[None] * states1, axis=1)).astype(jnp.bfloat16)
    states2 = li_decay[None] * states1 + zli1[:, None, :]
    yli1 = (li_qkv[1, 0].astype(jnp.float32) * jnp.sum(li_residue[None] * states2, axis=1)).astype(jnp.bfloat16)
    w_mr = full_matrix(mr_panels, panel_slot)
    w_li = full_matrix(li_panels, panel_slot)
    out0 = jnp.dot(ymr0, w_mr, preferred_element_type=jnp.float32) + jnp.dot(yli0, w_li, preferred_element_type=jnp.float32)
    out1 = jnp.dot(ymr1, w_mr, preferred_element_type=jnp.float32) + jnp.dot(yli1, w_li, preferred_element_type=jnp.float32)
    active0 = (remaining > 0).astype(jnp.float32)[:, None]
    active1 = (remaining > 1).astype(jnp.float32)[:, None]
    mixed = jnp.stack([out0 * active0, out1 * active1]).astype(jnp.bfloat16)
    return (mixed, new_tails, states2)
```

```python
import functools

import jax
import jax.numpy as jnp
from jax import lax
from jax.experimental import pallas as pl
from jax.experimental.pallas import tpu as pltpu
from jax.sharding import PartitionSpec as P

CAP = 2
BF = jnp.bfloat16
F32 = jnp.float32
ANY = pl.BlockSpec(memory_space=pl.ANY)
SM = pl.BlockSpec(memory_space=pltpu.SMEM)
VM = pl.BlockSpec(memory_space=pltpu.VMEM)
VLIM = 56 << 20


def lane_chunk(width):
    for size in (256, 128):
        if width % size == 0:
            return size
    return width


def links(engines):
    chips = engines // 2
    return [(k, f) for k in range(chips) for f in (0, 1)]


def send(x, engines, k, f):
    chips = engines // 2
    pairs = [(e, ((e // 2 + k) % chips) * 2 + ((e % 2) ^ f)) for e in range(engines)]
    return lax.ppermute(x, "engine", pairs)


def to_engine(me, k, f, engines):
    chips = engines // 2
    return ((me // 2 + k) % chips) * 2 + ((me % 2 + f) % 2)


def relation_of(me, owner, engines):
    chips = engines // 2
    k = (me // 2 + chips - owner // 2) % chips
    return 2 * k + (owner + me) % 2


def shifted_filters(filt_ref, f1, f2, width, chunk):
    taps = filt_ref.shape[0]
    for c in range(0, width, chunk):
        cols = pl.ds(c, chunk)
        f = filt_ref[:, cols].astype(F32)
        f1[0 : taps - 1, cols] = f[1:taps]
        f2[0 : taps - 2, cols] = f[2:taps]
        f2[taps - 2 : taps - 1, cols] = jnp.zeros((1, chunk), F32)


def pack_body(engines, rows, source, tails, states, filt, decay, resid, *refs):
    others = engines - 1
    count = others * CAP
    msgs = refs[: 1 + (others - 1) * CAP]
    parts = refs[len(msgs) : len(msgs) + others]
    f1, f2, tbuf, sbuf, mbuf, index, tsem, ssem, osem = refs[len(msgs) + others :]
    width = tails.shape[2]
    tail_len = tails.shape[1]
    modes = states.shape[1]
    chunk = lane_chunk(width)
    me = lax.axis_index("engine")
    rels = links(engines)
    order = [(rel, j) for rel in range(2, engines) for j in range(CAP)] + [(1, j) for j in range(CAP)]

    def fetch(rel, j):
        slot = (rel - 1) * CAP + j
        row = index[rel * (CAP + 1) + j]
        return (
            pltpu.make_async_copy(tails.at[row], tbuf.at[slot], tsem.at[slot]),
            pltpu.make_async_copy(states.at[row], sbuf.at[slot], ssem.at[slot]),
        )

    for rel in range(1, engines):
        k, f = rels[rel]
        there = to_engine(me, k, f, engines)
        for j in range(CAP):
            index[rel * (CAP + 1) + j] = 0

        def scan(i, found):
            old = source[there * rows + i]
            index[rel * (CAP + 1) + jnp.minimum(found, CAP)] = old % rows
            return found + jnp.where(old // rows == me, 1, 0)

        lax.fori_loop(0, rows, scan, 0)
    for rel, j in order:
        for copy in fetch(rel, j):
            copy.start()
    shifted_filters(filt, f1, f2, width, chunk)

    def target(rel, j):
        slot = (rel - 1) * CAP + j
        out = msgs[0].at[j] if rel == 1 else msgs[1 + (rel - 2) * CAP + j]
        return pltpu.make_async_copy(mbuf.at[slot], out, osem.at[slot])

    for rel, j in order:
        slot = (rel - 1) * CAP + j
        for copy in fetch(rel, j):
            copy.wait()

        def columns(c, carry):
            cols = pl.ds(pl.multiple_of(c * chunk, chunk), chunk)
            t = tbuf[slot, :, cols].astype(F32)
            parts[rel - 1][4 * j : 4 * j + 1, cols] = jnp.sum(t * f1[:, cols], axis=0, keepdims=True)
            parts[rel - 1][4 * j + 1 : 4 * j + 2, cols] = jnp.sum(t * f2[:, cols], axis=0, keepdims=True)
            mbuf[slot, 0:tail_len, cols] = jnp.concatenate(
                [jnp.zeros((2, chunk), F32), t[: tail_len - 2]], axis=0
            ).astype(BF)
            s = sbuf[slot, :, cols]
            d = decay[:, cols]
            a = resid[:, cols] * d * s
            parts[rel - 1][4 * j + 2 : 4 * j + 3, cols] = jnp.sum(a, axis=0, keepdims=True)
            parts[rel - 1][4 * j + 3 : 4 * j + 4, cols] = jnp.sum(a * d, axis=0, keepdims=True)
            mbuf[slot, tail_len + 1 : tail_len + 1 + modes, cols] = s.astype(BF)
            return carry

        lax.fori_loop(0, width // chunk, columns, 0)
        target(rel, j).start()
    for rel, j in order:
        target(rel, j).wait()


def keep_body(engines, rows, source, tails, states, filt, decay, resid, mr, li, new_tails, new_states, parts, gates,
              f1, f2, tbuf, sbuf, obuf, tsem, ssem, otsem, ossem):
    width = tails.shape[2]
    tail_len = tails.shape[1]
    chunk = lane_chunk(width)
    me = lax.axis_index("engine")

    def fetch(r):
        row = source[me * rows + r] % rows
        return (
            pltpu.make_async_copy(tails.at[row], tbuf.at[r], tsem.at[r]),
            pltpu.make_async_copy(states.at[row], sbuf.at[r], ssem.at[r]),
        )

    def store(r):
        return (
            pltpu.make_async_copy(obuf.at[r], new_tails.at[r], otsem.at[r]),
            pltpu.make_async_copy(sbuf.at[r], new_states.at[r], ossem.at[r]),
        )

    def stays(r):
        return source[me * rows + r] // rows == me

    def begin(r, carry):
        @pl.when(stays(r))
        def _():
            for copy in fetch(r):
                copy.start()

        return carry

    lax.fori_loop(0, rows, begin, 0)
    shifted_filters(filt, f1, f2, width, chunk)
    for c in range(0, width, chunk):
        cols = pl.ds(c, chunk)
        for step in range(2):
            gates[step, :, cols] = (
                (mr[step, 1, :, cols].astype(F32) * mr[step, 2, :, cols].astype(F32)).astype(BF).astype(F32)
            )
            gates[2 + step, :, cols] = (
                (li[step, 1, :, cols].astype(F32) * li[step, 2, :, cols].astype(F32)).astype(BF).astype(F32)
            )

    def work(r, carry):
        @pl.when(stays(r))
        def _():
            for copy in fetch(r):
                copy.wait()

            def columns(c, inner):
                cols = pl.ds(pl.multiple_of(c * chunk, chunk), chunk)
                one = pl.ds(r, 1)
                t = tbuf[r, :, cols].astype(F32)
                parts[0, one, cols] = jnp.sum(t * f1[:, cols], axis=0, keepdims=True)
                parts[1, one, cols] = jnp.sum(t * f2[:, cols], axis=0, keepdims=True)
                obuf[r, :, cols] = jnp.concatenate(
                    [gates[1, one, cols], gates[0, one, cols], t[: tail_len - 2]], axis=0
                ).astype(BF)
                s = sbuf[r, :, cols]
                d = decay[:, cols]
                w = resid[:, cols]
                ds = d * s
                parts[2, one, cols] = jnp.sum(w * ds, axis=0, keepdims=True)
                parts[3, one, cols] = jnp.sum(w * d * ds, axis=0, keepdims=True)
                sbuf[r, :, cols] = d * (ds + gates[2, one, cols]) + gates[3, one, cols]
                return inner

            lax.fori_loop(0, width // chunk, columns, 0)
            for copy in store(r):
                copy.start()

        return carry

    lax.fori_loop(0, rows, work, 0)

    def finish(r, carry):
        @pl.when(stays(r))
        def _():
            for copy in store(r):
                copy.wait()

        return carry

    lax.fori_loop(0, rows, finish, 0)


def arrivals(engines, rows, source, slots, found, me):
    for rel in range(engines):
        found[rel] = 0

    def scan(r, carry):
        rel = relation_of(me, source[me * rows + r] // rows, engines)
        at = found[rel]
        slots[rel * (CAP + 1) + jnp.minimum(at, CAP)] = r
        found[rel] = at + 1
        return carry

    lax.fori_loop(0, rows, scan, 0)


def mix_body(engines, rows, source, parts_in, gates, mr, li, filt, decay, resid, *refs):
    got = refs[: engines - 1]
    y, parts, slots, found = refs[engines - 1 :]
    width = y.shape[1]
    chunk = lane_chunk(width)
    me = lax.axis_index("engine")
    arrivals(engines, rows, source, slots, found, me)
    parts[...] = parts_in[...]
    for rel in range(1, engines):
        for j in range(CAP):

            @pl.when(found[rel] > j)
            def _():
                one = pl.ds(slots[rel * (CAP + 1) + j], 1)
                for i in range(4):
                    parts[i, one, :] = got[rel - 1][4 * j + i : 4 * j + i + 1, :].astype(F32)

    for c in range(0, width, chunk):
        cols = pl.ds(c, chunk)
        f = filt[0:16, cols].astype(F32)
        d = decay[:, cols]
        w = resid[:, cols]
        r0 = jnp.sum(w, axis=0, keepdims=True)
        r1 = jnp.sum(w * d, axis=0, keepdims=True)
        conv0 = f[0:1] * gates[0, :, cols] + parts[0, :, cols]
        conv1 = f[0:1] * gates[1, :, cols] + f[1:2] * gates[0, :, cols] + parts[1, :, cols]
        y[0:rows, cols] = (mr[0, 0, :, cols].astype(F32) * conv0).astype(BF)
        y[rows : 2 * rows, cols] = (mr[1, 0, :, cols].astype(F32) * conv1).astype(BF)
        modal0 = parts[2, :, cols] + gates[2, :, cols] * r0
        modal1 = parts[3, :, cols] + gates[2, :, cols] * r1 + gates[3, :, cols] * r0
        y[2 * rows : 3 * rows, cols] = (li[0, 0, :, cols].astype(F32) * modal0).astype(BF)
        y[3 * rows : 4 * rows, cols] = (li[1, 0, :, cols].astype(F32) * modal1).astype(BF)


def project_body(engines, rows, slots_here, depth, *refs):
    ys = refs[:engines]
    mr_w, li_w = refs[engines : engines + 2]
    outs = refs[engines + 2 : 2 * engines + 2]
    x, acc = refs[2 * engines + 2 :]
    two = 2 * rows
    width = ys[0].shape[1]
    pw = mr_w.shape[2]
    step = pl.program_id(0)

    @pl.when(step == 0)
    def _():
        for rel in range(engines):
            for b in range(width // depth):
                x[b, 0, rel * two : (rel + 1) * two, :] = ys[rel][0:two, b * depth : (b + 1) * depth]
                x[b, 1, rel * two : (rel + 1) * two, :] = ys[rel][two : 2 * two, b * depth : (b + 1) * depth]
        acc[...] = jnp.zeros_like(acc)

    for g in range(slots_here):
        cols = slice(g * pw, (g + 1) * pw)
        acc[:, cols] += jnp.dot(x[step, 0], mr_w[g], preferred_element_type=F32) + jnp.dot(
            x[step, 1], li_w[g], preferred_element_type=F32
        )

    @pl.when(step == pl.num_programs(0) - 1)
    def _():
        for rel in range(engines):
            outs[rel][...] = acc[rel * two : (rel + 1) * two, :].astype(BF)


def sort_body(engines, chans, slots_here, slot_of, *refs):
    got = refs[:engines]
    outs = refs[engines : engines + chans]
    tiles = refs[engines + chans]
    pw = tiles.shape[2]
    me = lax.axis_index("engine")
    here = lax.axis_index("chan")
    per_chan = slot_of.shape[0] // chans
    for rel in range(engines):
        for g in range(slots_here):
            tiles[rel * slots_here + g] = got[rel][:, g * pw : (g + 1) * pw]
    for d in range(chans):
        there = (here + d) % chans
        for h in range(per_chan):
            slot = slot_of[there * per_chan + h]
            rel = relation_of(me, slot // slots_here, engines)
            outs[d][:, h * pw : (h + 1) * pw] = tiles[rel * slots_here + slot % slots_here]


def place_body(engines, rows, items, source, gates, decay, *refs):
    msgs = refs[: len(items)]
    old_tails, old_states = refs[len(items) : len(items) + 2]
    new_tails, new_states = refs[len(items) + 2 : len(items) + 4]
    mbuf, obuf, sbuf, slots, found, isem, osem, ssem = refs[len(items) + 4 :]
    tail_len = new_tails.shape[1]
    width = new_tails.shape[2]
    modes = new_states.shape[1]
    chunk = lane_chunk(width)
    me = lax.axis_index("engine")

    def inbound(n):
        return pltpu.make_async_copy(msgs[n], mbuf.at[n], isem.at[n])

    def outbound(n, row):
        return (
            pltpu.make_async_copy(obuf.at[n], new_tails.at[row], osem.at[n]),
            pltpu.make_async_copy(sbuf.at[n], new_states.at[row], ssem.at[n]),
        )

    for n in range(len(items)):
        inbound(n).start()
    arrivals(engines, rows, source, slots, found, me)
    for n, (rel, j) in enumerate(items):
        inbound(n).wait()

        @pl.when(found[rel] > j)
        def _():
            row = slots[rel * (CAP + 1) + j]
            one = pl.ds(row, 1)

            def columns(c, carry):
                cols = pl.ds(pl.multiple_of(c * chunk, chunk), chunk)
                obuf[n, :, cols] = mbuf[n, 0:tail_len, cols]
                obuf[n, 0:2, cols] = jnp.concatenate([gates[1, one, cols], gates[0, one, cols]], axis=0).astype(BF)
                s = mbuf[n, tail_len + 1 : tail_len + 1 + modes, cols].astype(F32)
                d = decay[:, cols]
                sbuf[n, :, cols] = d * (d * s + gates[2, one, cols]) + gates[3, one, cols]
                return carry

            lax.fori_loop(0, width // chunk, columns, 0)
            for copy in outbound(n, row):
                copy.start()

    for n, (rel, j) in enumerate(items):

        @pl.when(found[rel] > j)
        def _():
            for copy in outbound(n, slots[rel * (CAP + 1) + j]):
                copy.wait()


def body(mr_qkv, li_qkv, conv_tails, modal_states, source, remaining, mr_filter, li_decay, li_residue, mr_panels,
         li_panels, panel_slot):
    engines = lax.axis_size("engine")
    chans = lax.axis_size("chan")
    rows, tail_len, width = conv_tails.shape
    modes = modal_states.shape[1]
    taps = mr_filter.shape[0]
    slots_here, _, pw = mr_panels.shape
    others = engines - 1
    count = others * CAP
    chips = engines // 2
    rels = links(engines)
    msg_rows = tail_len + 1 + modes
    sds = jax.ShapeDtypeStruct
    dma = pltpu.SemaphoreType.DMA
    params = pltpu.CompilerParams(vmem_limit_bytes=VLIM)

    cross = [(rel, j) for rel in range(2, engines) for j in range(CAP)]
    packed = pl.pallas_call(
        functools.partial(pack_body, engines, rows),
        in_specs=[SM, ANY, ANY, VM, VM, VM],
        out_specs=[ANY] * (1 + len(cross)) + [VM] * others,
        out_shape=[sds((CAP, msg_rows, width), BF)]
        + [sds((msg_rows, width), BF)] * len(cross)
        + [sds((4 * CAP, width), F32)] * others,
        scratch_shapes=[
            pltpu.VMEM((taps - 1, width), F32),
            pltpu.VMEM((taps - 1, width), F32),
            pltpu.VMEM((count, tail_len, width), BF),
            pltpu.VMEM((count, modes, width), F32),
            pltpu.VMEM((count, msg_rows, width), BF),
            pltpu.SMEM((engines * (CAP + 1),), jnp.int32),
            dma((count,)),
            dma((count,)),
            dma((count,)),
        ],
        compiler_params=params,
        name="pack",
    )(source, conv_tails, modal_states, mr_filter, li_decay, li_residue)
    near_msg = packed[0]
    far_msgs = packed[1 : 1 + len(cross)]
    parts_out = packed[1 + len(cross) :]

    quarter = (len(cross) + 3) // 4
    batch = [list(range(i * quarter, min((i + 1) * quarter, len(cross)))) for i in range(4)]
    far_got = {}

    def launch(group, token=None):
        for n in group:
            msg = far_msgs[n]
            if token is not None:
                msg, _ = lax.optimization_barrier((msg, token))
            k, f = rels[cross[n][0]]
            far_got[n] = send(msg, engines, k, f)

    parts_got = [send(parts_out[rel - 1], engines, *rels[rel]) for rel in range(1, engines)]
    launch(batch[0])
    near_got = send(near_msg, engines, 0, 1)

    new_tails, new_states, parts, gates = pl.pallas_call(
        functools.partial(keep_body, engines, rows),
        in_specs=[SM, ANY, ANY, VM, VM, VM, VM, VM],
        out_specs=[ANY, ANY, VM, VM],
        out_shape=[
            sds((rows, tail_len, width), BF),
            sds((rows, modes, width), F32),
            sds((4, rows, width), F32),
            sds((4, rows, width), F32),
        ],
        scratch_shapes=[
            pltpu.VMEM((taps - 1, width), F32),
            pltpu.VMEM((taps - 1, width), F32),
            pltpu.VMEM((rows, tail_len, width), BF),
            pltpu.VMEM((rows, modes, width), F32),
            pltpu.VMEM((rows, tail_len, width), BF),
            dma((rows,)),
            dma((rows,)),
            dma((rows,)),
            dma((rows,)),
        ],
        compiler_params=params,
        name="keep",
    )(source, conv_tails, modal_states, mr_filter, li_decay, li_residue, mr_qkv, li_qkv)
    launch(batch[1], gates[0, 0, 0])

    y = pl.pallas_call(
        functools.partial(mix_body, engines, rows),
        in_specs=[SM] + [VM] * 7 + [VM] * others,
        out_specs=VM,
        out_shape=sds((4 * rows, width), BF),
        scratch_shapes=[
            pltpu.VMEM((4, rows, width), F32),
            pltpu.SMEM((engines * (CAP + 1),), jnp.int32),
            pltpu.SMEM((engines,), jnp.int32),
        ],
        compiler_params=params,
        name="mix",
    )(source, parts, gates, mr_qkv, li_qkv, mr_filter, li_decay, li_residue, *parts_got)

    same_core = [y] + [send(y, engines, k, 0) for k in range(1, chips)]
    launch(batch[2], y[0, 0])
    ys = []
    for k in range(chips):
        ys += [same_core[k], send(same_core[k], engines, 0, 1)]

    depth = 512
    outs = pl.pallas_call(
        functools.partial(project_body, engines, rows, slots_here, depth),
        grid=(width // depth,),
        in_specs=[pl.BlockSpec((4 * rows, width), lambda i: (0, 0))] * engines
        + [pl.BlockSpec((slots_here, depth, pw), lambda i: (0, i, 0))] * 2,
        out_specs=[pl.BlockSpec((2 * rows, slots_here * pw), lambda i: (0, 0))] * engines,
        out_shape=[sds((2 * rows, slots_here * pw), BF)] * engines,
        scratch_shapes=[
            pltpu.VMEM((width // depth, 2, engines * 2 * rows, depth), BF),
            pltpu.VMEM((engines * 2 * rows, slots_here * pw), F32),
        ],
        compiler_params=params,
        name="project",
    )(*ys, mr_panels, li_panels)

    back = [outs[0]]
    for k, f in rels[1:]:
        back.append(send(outs[2 * ((chips - k) % chips) + f], engines, k, f))
    launch(batch[3], outs[0][0, 0])

    per_chan = panel_slot.shape[0] // chans
    blocks = pl.pallas_call(
        functools.partial(sort_body, engines, chans, slots_here),
        in_specs=[SM] + [VM] * engines,
        out_specs=[VM] * chans,
        out_shape=[sds((2 * rows, per_chan * pw), BF)] * chans,
        scratch_shapes=[pltpu.VMEM((engines * slots_here, 2 * rows, pw), BF)],
        compiler_params=params,
        name="sort",
    )(panel_slot, *back)
    total = blocks[0].astype(F32)
    for d in range(1, chans):
        total = total + lax.ppermute(blocks[d], "chan", [(c, (c + d) % chans) for c in range(chans)]).astype(F32)
    steps_ids = jnp.arange(2, dtype=jnp.int32)
    active = (remaining[None, :] > steps_ids[:, None]).astype(F32)
    mixed = (total.reshape(2, rows, per_chan * pw) * active[:, :, None]).astype(BF)

    def place(items, arrays, tails, states):
        return pl.pallas_call(
            functools.partial(place_body, engines, rows, items),
            in_specs=[SM, VM, VM] + [ANY] * (len(items) + 2),
            out_specs=[ANY, ANY],
            out_shape=[sds(tails.shape, BF), sds(states.shape, F32)],
            input_output_aliases={3 + len(items): 0, 4 + len(items): 1},
            scratch_shapes=[
                pltpu.VMEM((len(items), msg_rows, width), BF),
                pltpu.VMEM((len(items), tail_len, width), BF),
                pltpu.VMEM((len(items), modes, width), F32),
                pltpu.SMEM((engines * (CAP + 1),), jnp.int32),
                pltpu.SMEM((engines,), jnp.int32),
                dma((len(items),)),
                dma((len(items),)),
                dma((len(items),)),
            ],
            compiler_params=params,
            name="place",
        )(source, gates, li_decay, *arrays, tails, states)

    new_tails, new_states = place(
        [(1, j) for j in range(CAP)], [near_got[j] for j in range(CAP)], new_tails, new_states
    )
    for group in batch:
        if group:
            new_tails, new_states = place([cross[n] for n in group], [far_got[n] for n in group], new_tails, new_states)
    return (mixed, new_tails, new_states)


def solution(mesh):
    return jax.shard_map(
        body,
        mesh=mesh,
        in_specs=(
            P(None, None, ("group", "engine"), "chan"),
            P(None, None, ("group", "engine"), "chan"),
            P(("group", "engine"), None, "chan"),
            P(("group", "engine"), None, "chan"),
            P("group"),
            P(("group", "engine")),
            P(None, "chan"),
            P(None, "chan"),
            P(None, "chan"),
            P("engine", "chan", None),
            P("engine", "chan", None),
            P(),
        ),
        out_specs=(
            P(None, ("group", "engine"), "chan"),
            P(("group", "engine"), None, "chan"),
            P(("group", "engine"), None, "chan"),
        ),
        check_vma=False,
    )
```

```python
import functools

import jax
import jax.numpy as jnp
from jax import lax
from jax.experimental import pallas as pl
from jax.experimental.pallas import tpu as pltpu
from jax.sharding import PartitionSpec as P

CAP = 2
BF = jnp.bfloat16
F32 = jnp.float32
ANY = pl.BlockSpec(memory_space=pl.ANY)
SM = pl.BlockSpec(memory_space=pltpu.SMEM)
VM = pl.BlockSpec(memory_space=pltpu.VMEM)
VLIM = 48 << 20
TB = 16
TINY = pl.CostEstimate(flops=1, transcendentals=0, bytes_accessed=1)


def lane_chunk(width):
    for size in (256, 128):
        if width % size == 0:
            return size
    return width


def wide_chunk(width):
    return 1024 if width % 1024 == 0 else lane_chunk(width)


def links(engines):
    chips = engines // 2
    return [(k, f) for k in range(chips) for f in (0, 1)]


def send(x, engines, k, f):
    chips = engines // 2
    pairs = [(e, ((e // 2 + k) % chips) * 2 + ((e % 2) ^ f)) for e in range(engines)]
    return lax.ppermute(x, "engine", pairs)


def to_engine(me, k, f, engines):
    chips = engines // 2
    return lax.rem(lax.div(me, 2) + k, chips) * 2 + lax.rem(me + f, 2)


def relation_of(me, owner, engines):
    chips = engines // 2
    k = lax.rem(lax.div(me, 2) + chips - lax.div(owner, 2), chips)
    return 2 * k + lax.rem(owner + me, 2)


def departures(engines, rows, source, leave, me):
    for rel, (k, f) in enumerate(links(engines)):
        if rel == 0:
            continue
        there = to_engine(me, k, f, engines)
        for j in range(CAP):
            leave[rel * (CAP + 1) + j] = 0

        found = 0
        for i in range(rows):
            old = source[there * rows + i]
            leave[rel * (CAP + 1) + jnp.minimum(found, CAP)] = lax.rem(old, rows)
            found = found + jnp.where(lax.div(old, rows) == me, 1, 0)


def send_selector(rels, rows, leave, pick):
    height, depth = pick.shape
    at = lax.broadcasted_iota(jnp.int32, (height, 1), 0)
    group = at // (TB * CAP)
    tap = (at % (TB * CAP)) // CAP
    place = at % CAP
    row = jnp.zeros((height, 1), jnp.int32)
    for i, rel in enumerate(rels):
        for j in range(CAP):
            row = jnp.where((group == i) & (place == j), leave[rel * (CAP + 1) + j], row)
    want = tap * rows + row
    pick[...] = (lax.broadcasted_iota(jnp.int32, (height, depth), 1) == want).astype(F32).astype(BF)


def sent_taps(b, tail_len):
    return min(TB, tail_len - 2 - b * TB)


def early_body(engines, rows, blocks, source, tails, *refs):
    far = list(range(2, engines))
    msgs = refs[: len(far)]
    tbuf, pick, leave, tsem = refs[len(far) :]
    tail_len, _, width = tails.shape
    chunk = wide_chunk(width)
    me = lax.axis_index("engine")

    def fetch(n):
        return pltpu.make_async_copy(tails.at[pl.ds(blocks[n] * TB, TB)], tbuf.at[pl.ds(n * TB, TB)], tsem.at[n])

    for n in range(len(blocks)):
        fetch(n).start()
    departures(engines, rows, source, leave, me)
    send_selector(far, rows, leave, pick)
    for n in range(len(blocks)):
        fetch(n).wait()

        for c in range(0, width, chunk):
            cols = pl.ds(c, chunk)
            old = tbuf[n * TB : (n + 1) * TB, :, cols].reshape(TB * rows, chunk)
            rowsel = jnp.dot(pick[...], old, preferred_element_type=F32).astype(BF)
            for i in range(len(far)):
                msgs[i][n * TB * CAP : (n + 1) * TB * CAP, cols] = rowsel[i * TB * CAP : (i + 1) * TB * CAP]


def lead_body(engines, rows, source, tails, states, filt, decay, resid, _, *refs):
    others = engines - 1
    parts = refs[0]
    small = refs[1 : 1 + others]
    fbuf, tbuf, sbuf, leave, tsem, ssem = refs[1 + others :]
    tail_len, _, width = tails.shape
    modes = states.shape[1]
    taps = filt.shape[0]
    chunk = wide_chunk(width)
    me = lax.axis_index("engine")
    total = pl.cdiv(tail_len, TB)

    def fetch(b):
        size = min(TB, tail_len - b * TB)
        return pltpu.make_async_copy(
            tails.at[pl.ds(b * TB, size)], tbuf.at[pl.ds(b * TB, size)], tsem.at[b]
        )

    for b in range(total):
        fetch(b).start()
    load_states = pltpu.make_async_copy(states, sbuf, ssem)
    load_states.start()
    departures(engines, rows, source, leave, me)
    for c in range(0, width, chunk):
        fbuf[0:taps, pl.ds(c, chunk)] = filt[:, pl.ds(c, chunk)].astype(F32)
        fbuf[taps : taps + 8, pl.ds(c, chunk)] = jnp.zeros((8, chunk), F32)
    for b in range(total):
        fetch(b).wait()
        size = min(TB, tail_len - b * TB)

        for c in range(0, width, chunk):
            cols = pl.ds(c, chunk)
            if b == 0:
                first = jnp.zeros((rows, chunk), F32)
                second = jnp.zeros((rows, chunk), F32)
            else:
                first = parts[0, :, cols]
                second = parts[1, :, cols]
            for i in range(size):
                t = tbuf[b * TB + i, :, cols].astype(F32)
                first += t * fbuf[b * TB + i + 1 : b * TB + i + 2, cols]
                second += t * fbuf[b * TB + i + 2 : b * TB + i + 3, cols]
            parts[0, :, cols] = first
            parts[1, :, cols] = second
    load_states.wait()

    def modal(r, carry):
        s = sbuf[r]
        a = resid[...] * (decay[...] * s)
        parts[2, pl.ds(r, 1), :] = jnp.sum(a, axis=0, keepdims=True)
        parts[3, pl.ds(r, 1), :] = jnp.sum(a * decay[...], axis=0, keepdims=True)
        return carry

    lax.fori_loop(0, rows, modal, 0)
    for rel in range(1, engines):
        for j in range(CAP):
            one = pl.ds(leave[rel * (CAP + 1) + j], 1)
            for i in range(4):
                small[rel - 1][4 * j + i : 4 * j + i + 1, :] = parts[i, one, :].astype(small[rel - 1].dtype)


def pack_body(engines, rows, chunks, state_chunk, source, tails, states, _, *refs):
    far = list(range(2, engines))
    near = refs[0]
    msgs = refs[1 : 1 + len(far) * len(chunks)]
    spread, tbuf, sbuf, pick, leave, slots, found, tsem, ssem = refs[1 + len(msgs) :]
    tail_len, _, width = tails.shape
    modes = states.shape[1]
    chunk = wide_chunk(width)
    me = lax.axis_index("engine")
    total = pl.cdiv(tail_len - 2, TB)
    others = engines - 1

    def fetch(b):
        n = sent_taps(b, tail_len)
        return pltpu.make_async_copy(tails.at[pl.ds(b * TB, n)], tbuf.at[pl.ds(b * TB, n)], tsem.at[b])

    def fetch_state(rel, j):
        slot = (rel - 1) * CAP + j
        return pltpu.make_async_copy(states.at[leave[rel * (CAP + 1) + j]], sbuf.at[slot], ssem.at[slot])

    for b in range(total):
        fetch(b).start()
    departures(engines, rows, source, leave, me)
    for rel in range(1, engines):
        for j in range(CAP):
            fetch_state(rel, j).start()
    send_selector([1] + far, rows, leave, pick)
    arrivals(engines, rows, source, slots, found, me)
    height, depth = spread.shape
    at = lax.broadcasted_iota(jnp.int32, (height, 1), 0)
    tap = at // rows
    new_row = at % rows
    want = jnp.zeros((height, 1), jnp.int32)
    for r in range(rows):
        old = source[me * rows + r]
        want = jnp.where(new_row == r, tap * rows + old % rows, want)
    for rel in range(1, engines):
        for j in range(CAP):
            row = jnp.where(found[rel] > j, slots[rel * (CAP + 1) + j], -1)
            want = jnp.where(new_row == row, TB * rows + (rel - 1) * TB * CAP + CAP * tap + j, want)
    spread[...] = (lax.broadcasted_iota(jnp.int32, (height, depth), 1) == want).astype(F32).astype(BF)
    for b in range(total):
        fetch(b).wait()
        n = sent_taps(b, tail_len)
        home = [i for i, blocks in enumerate(chunks) if b in blocks]
        tall = pick.shape[0] if home else TB * CAP

        for c in range(0, width, chunk):
            cols = pl.ds(c, chunk)
            old = tbuf[b * TB : b * TB + n, :, cols].reshape(n * rows, chunk)
            rowsel = jnp.dot(pick[0:tall, 0 : n * rows], old, preferred_element_type=F32).astype(BF)
            near[b * TB * CAP : (b + 1) * TB * CAP, cols] = rowsel[0 : TB * CAP]
            if home:
                base = (b - chunks[home[0]][0]) * TB * CAP
                for i in range(len(far)):
                    msgs[home[0] * len(far) + i][base : base + TB * CAP, cols] = rowsel[
                        (i + 1) * TB * CAP : (i + 2) * TB * CAP
                    ]
    for rel in range(1, engines):
        for j in range(CAP):
            fetch_state(rel, j).wait()
            slot = (rel - 1) * CAP + j
            if rel == 1:
                base = total * TB * CAP
                near[base + j * modes : base + (j + 1) * modes, :] = sbuf[slot].astype(BF)
            else:
                base = len(chunks[state_chunk]) * TB * CAP
                msgs[state_chunk * len(far) + rel - 2][base + j * modes : base + (j + 1) * modes, :] = sbuf[
                    slot
                ].astype(BF)


def arrivals(engines, rows, source, slots, found, me):
    for rel in range(engines):
        found[rel] = 0
    for r in range(rows):
        rel = relation_of(me, lax.div(source[me * rows + r], rows), engines)
        at = found[rel]
        slots[rel * (CAP + 1) + jnp.minimum(at, CAP)] = r
        found[rel] = at + 1


def mix_body(engines, rows, source, parts_in, mr, li, filt, decay, resid, *refs):
    got = refs[: engines - 1]
    y, gates, parts, slots, found = refs[-5:]
    width = y.shape[1]
    chunk = lane_chunk(width)
    me = lax.axis_index("engine")
    arrivals(engines, rows, source, slots, found, me)

    def stay(r, carry):
        old = source[me * rows + r] % rows
        for i in range(4):
            parts[i, pl.ds(r, 1), :] = parts_in[i, pl.ds(old, 1), :]
        return carry

    lax.fori_loop(0, rows, stay, 0)
    for rel in range(1, engines):
        for j in range(CAP):

            @pl.when(found[rel] > j)
            def _():
                one = pl.ds(slots[rel * (CAP + 1) + j], 1)
                for i in range(4):
                    parts[i, one, :] = got[rel - 1][4 * j + i : 4 * j + i + 1, :].astype(F32)

    for c in range(0, width, chunk):
        cols = pl.ds(c, chunk)
        f = filt[0:16, cols].astype(F32)
        d = decay[:, cols]
        w = resid[:, cols]
        r0 = jnp.sum(w, axis=0, keepdims=True)
        r1 = jnp.sum(w * d, axis=0, keepdims=True)
        z = []
        for n, qkv in enumerate((mr, mr, li, li)):
            gate = (qkv[n % 2, 1, :, cols].astype(F32) * qkv[n % 2, 2, :, cols].astype(F32)).astype(BF)
            gates[n, :, cols] = gate
            z.append(gate.astype(F32))
        conv0 = f[0:1] * z[0] + parts[0, :, cols]
        conv1 = f[0:1] * z[1] + f[1:2] * z[0] + parts[1, :, cols]
        y[0:rows, cols] = (mr[0, 0, :, cols].astype(F32) * conv0).astype(BF)
        y[rows : 2 * rows, cols] = (mr[1, 0, :, cols].astype(F32) * conv1).astype(BF)
        modal0 = parts[2, :, cols] + z[2] * r0
        modal1 = parts[3, :, cols] + z[2] * r1 + z[3] * r0
        y[2 * rows : 3 * rows, cols] = (li[0, 0, :, cols].astype(F32) * modal0).astype(BF)
        y[3 * rows : 4 * rows, cols] = (li[1, 0, :, cols].astype(F32) * modal1).astype(BF)


def project_body(engines, rows, slots_here, depth, *refs):
    ys = refs[:engines]
    mr_w, li_w = refs[engines : engines + 2]
    outs = refs[-2 - engines : -2]
    x, acc = refs[-2:]
    two = 2 * rows
    width = ys[0].shape[1]
    pw = mr_w.shape[2]
    step = pl.program_id(0)

    @pl.when(step == 0)
    def _():
        for rel in range(engines):
            for b in range(width // depth):
                x[b, 0, rel * two : (rel + 1) * two, :] = ys[rel][0:two, b * depth : (b + 1) * depth]
                x[b, 1, rel * two : (rel + 1) * two, :] = ys[rel][two : 2 * two, b * depth : (b + 1) * depth]
        acc[...] = jnp.zeros_like(acc)

    for g in range(slots_here):
        cols = slice(g * pw, (g + 1) * pw)
        acc[:, cols] += jnp.dot(x[step, 0], mr_w[g], preferred_element_type=F32) + jnp.dot(
            x[step, 1], li_w[g], preferred_element_type=F32
        )

    @pl.when(step == pl.num_programs(0) - 1)
    def _():
        for rel in range(engines):
            outs[rel][...] = acc[rel * two : (rel + 1) * two, :].astype(BF)


def sort_body(engines, chans, slots_here, slot_of, *refs):
    got = refs[:engines]
    outs = refs[-1 - chans : -1]
    tiles = refs[-1]
    pw = tiles.shape[2]
    me = lax.axis_index("engine")
    here = lax.axis_index("chan")
    per_chan = slot_of.shape[0] // chans
    for rel in range(engines):
        for g in range(slots_here):
            tiles[rel * slots_here + g] = got[rel][:, g * pw : (g + 1) * pw]
    for d in range(chans):
        there = (here + d) % chans
        for h in range(per_chan):
            slot = slot_of[there * per_chan + h]
            rel = relation_of(me, slot // slots_here, engines)
            outs[d][:, h * pw : (h + 1) * pw] = tiles[rel * slots_here + slot % slots_here]


def place_body(engines, rows, blocks, spread, gates, tails, near, *refs):
    others = engines - 1
    msgs = refs[: others - 1]
    new_tails = refs[others]
    tbuf, mbuf, obuf, isem, osem = refs[others + 1 :]
    tail_len, _, width = tails.shape
    chunk = lane_chunk(width)
    first = blocks[0] == 0
    lead = 2 if first else 0

    def fetch(n):
        b = blocks[n]
        taps = sent_taps(b, tail_len)
        copies = [pltpu.make_async_copy(tails.at[pl.ds(b * TB, taps)], tbuf.at[n, pl.ds(0, taps)], isem.at[n, 0])]
        for rel in range(1, engines):
            ref = near if rel == 1 else msgs[rel - 2]
            base = (b if rel == 1 else n) * TB * CAP
            copies.append(
                pltpu.make_async_copy(ref.at[pl.ds(base, TB * CAP)], mbuf.at[n, rel - 1], isem.at[n, rel])
            )
        return copies

    def store(n):
        b = blocks[n]
        taps = sent_taps(b, tail_len)
        extra = lead if n == 0 else 0
        return pltpu.make_async_copy(
            obuf.at[n, pl.ds(2 - extra, taps + extra)], new_tails.at[pl.ds(b * TB + 2 - extra, taps + extra)], osem.at[n]
        )

    for n in range(len(blocks)):
        for copy in fetch(n):
            copy.start()
    for n, b in enumerate(blocks):
        for copy in fetch(n):
            copy.wait()
        taps = sent_taps(b, tail_len)
        if first and n == 0:
            obuf[0, 0] = gates[1]
            obuf[0, 1] = gates[0]

        for c in range(0, width, chunk):
            cols = pl.ds(c, chunk)
            old = tbuf[n, 0:taps, :, cols].reshape(taps * rows, chunk)
            got = jnp.concatenate([mbuf[n, i, :, cols] for i in range(others)], axis=0)
            top = taps * rows
            new = jnp.dot(spread[0:top, 0:top], old, preferred_element_type=F32) + jnp.dot(
                spread[0:top, TB * rows :], got, preferred_element_type=F32
            )
            obuf[n, 2 : 2 + taps, :, cols] = new.astype(BF).reshape(taps, rows, chunk)
        store(n).start()
    for n in range(len(blocks)):
        store(n).wait()


def modal_body(engines, rows, bases, source, states, gates, decay, near, *refs):
    others = engines - 1
    msgs = refs[: others - 1]
    new_states = refs[others - 1]
    sbuf, mbuf, slots, found, isem, msem, osem = refs[others:]
    modes = states.shape[1]
    width = states.shape[2]
    chunk = lane_chunk(width)
    me = lax.axis_index("engine")

    def fetch(r):
        return pltpu.make_async_copy(states.at[source[me * rows + r] % rows], sbuf.at[r], isem.at[r])

    def arrive(rel):
        ref = near if rel == 1 else msgs[rel - 2]
        return pltpu.make_async_copy(ref.at[pl.ds(bases[min(rel, 2) - 1], CAP * modes)], mbuf.at[rel - 1], msem.at[rel - 1])

    def store(r):
        return pltpu.make_async_copy(sbuf.at[r], new_states.at[r], osem.at[r])

    for r in range(rows):
        fetch(r).start()
    for rel in range(1, engines):
        arrive(rel).start()
    arrivals(engines, rows, source, slots, found, me)
    for r in range(rows):
        fetch(r).wait()
    for rel in range(1, engines):
        arrive(rel).wait()
        for j in range(CAP):

            @pl.when(found[rel] > j)
            def _():
                sbuf[slots[rel * (CAP + 1) + j]] = mbuf[rel - 1, j * modes : (j + 1) * modes].astype(F32)

    for r in range(rows):
        for c in range(0, width, chunk):
            cols = pl.ds(c, chunk)
            d = decay[:, cols]
            z0 = gates[2, r : r + 1, cols].astype(F32)
            z1 = gates[3, r : r + 1, cols].astype(F32)
            sbuf[r, :, cols] = d * (d * sbuf[r, :, cols] + z0) + z1
        store(r).start()
    for r in range(rows):
        store(r).wait()


def split(total):
    cuts = [0, 3 * total // 8, 5 * total // 8, total]
    return [list(range(a, b)) for a, b in zip(cuts, cuts[1:]) if a < b]


def body(mr_qkv, li_qkv, conv_tails, modal_states, source, remaining, mr_filter, li_decay, li_residue, mr_panels,
         li_panels, panel_slot):
    engines = lax.axis_size("engine")
    chans = lax.axis_size("chan")
    rows, tail_len, width = conv_tails.shape
    modes = modal_states.shape[1]
    taps = mr_filter.shape[0]
    slots_here, _, pw = mr_panels.shape
    others = engines - 1
    chips = engines // 2
    rels = links(engines)
    far = list(range(2, engines))
    sds = jax.ShapeDtypeStruct
    dma = pltpu.SemaphoreType.DMA
    params = pltpu.CompilerParams(vmem_limit_bytes=VLIM)
    tails = jnp.transpose(conv_tails, (1, 0, 2))
    blocks = pl.cdiv(tail_len - 2, TB)
    chunks = split(blocks)
    state_chunk = len(chunks) - 2
    table = pltpu.SMEM((engines * (CAP + 1),), jnp.int32)
    tally = pltpu.SMEM((engines,), jnp.int32)

    def msg_rows(i):
        return len(chunks[i]) * TB * CAP + (CAP * modes if i == state_chunk else 0)

    msgs = {}
    msgs[0] = pl.pallas_call(
        functools.partial(early_body, engines, rows, chunks[0]),
        in_specs=[SM, ANY],
        out_specs=[VM] * len(far),
        out_shape=[sds((msg_rows(0), width), BF)] * len(far),
        scratch_shapes=[
            pltpu.VMEM((len(chunks[0]) * TB, rows, width), BF),
            pltpu.VMEM((len(far) * TB * CAP, TB * rows), BF),
            table,
            dma((len(chunks[0]),)),
        ],
        compiler_params=params,
        name="early",
    )(source, tails)
    got = {}

    def launch(i, token=None):
        arrays = list(msgs[i])
        if token is not None:
            arrays, token = lax.optimization_barrier((arrays, token))
        got[i] = [send(a, engines, *rels[rel]) for a, rel in zip(arrays, far)]
        return token

    launch(0)
    lead = pl.pallas_call(
        functools.partial(lead_body, engines, rows),
        in_specs=[SM, ANY, ANY, VM, VM, VM, ANY],
        out_specs=[VM] * (1 + others),
        out_shape=[sds((4, rows, width), F32)] + [sds((4 * CAP, width), BF)] * others,
        scratch_shapes=[
            pltpu.VMEM((taps + 8, width), F32),
            pltpu.VMEM((tail_len, rows, width), BF),
            pltpu.VMEM((rows, modes, width), F32),
            table,
            dma((pl.cdiv(tail_len, TB),)),
            dma(()),
        ],
        compiler_params=params,
        name="lead",
    )(source, tails, modal_states, mr_filter, li_decay, li_residue, msgs[0][0])
    parts = lead[0]
    small = lead[1 : 1 + others]
    parts_got = [send(small[rel - 1], engines, *rels[rel]) for rel in range(1, engines)]

    later = chunks[1:]
    packed = pl.pallas_call(
        functools.partial(pack_body, engines, rows, later, state_chunk - 1),
        in_specs=[SM, ANY, ANY, ANY],
        out_specs=[VM] * (2 + len(far) * len(later)),
        out_shape=[sds((blocks * TB * CAP + CAP * modes, width), BF)]
        + [sds((msg_rows(i), width), BF) for i in range(1, len(chunks)) for _ in far]
        + [sds((TB * rows, TB * rows + others * TB * CAP), BF)],
        scratch_shapes=[
            pltpu.VMEM((tail_len, rows, width), BF),
            pltpu.VMEM((others * CAP, modes, width), F32),
            pltpu.VMEM((others * TB * CAP, TB * rows), BF),
            table,
            table,
            tally,
            dma((blocks,)),
            dma((others * CAP,)),
        ],
        compiler_params=params,
        name="pack",
    )(source, tails, modal_states, small[0])
    near_msg = packed[0]
    spread = packed[-1]
    for i in range(1, len(chunks)):
        msgs[i] = packed[1 + (i - 1) * len(far) : 1 + i * len(far)]

    y, gates = pl.pallas_call(
        functools.partial(mix_body, engines, rows),
        in_specs=[SM] + [VM] * (6 + others) + [ANY] * (1 + len(far)),
        out_specs=[VM, VM],
        out_shape=[sds((4 * rows, width), BF), sds((4, rows, width), BF)],
        scratch_shapes=[pltpu.VMEM((4, rows, width), F32), table, tally],
        compiler_params=params,
        name="mix",
    )(source, parts, mr_qkv, li_qkv, mr_filter, li_decay, li_residue, *parts_got, spread, *got[0])

    near_msg, y = lax.optimization_barrier((near_msg, y))
    near_got = send(near_msg, engines, 0, 1)
    same_core = [y] + [send(y, engines, k, 0) for k in range(1, chips)]
    ys = []
    for k in range(chips):
        ys += [same_core[k], send(same_core[k], engines, 0, 1)]
    ys[1] = launch(1, ys[1])

    def place(i, new_tails):
        return pl.pallas_call(
            functools.partial(place_body, engines, rows, chunks[i]),
            in_specs=[VM, VM] + [ANY] * (2 + len(far) + 1),
            out_specs=ANY,
            out_shape=sds((tail_len, rows, width), BF),
            input_output_aliases={} if i == 0 else {4 + len(far): 0},
            scratch_shapes=[
                pltpu.VMEM((len(chunks[i]), TB, rows, width), BF),
                pltpu.VMEM((len(chunks[i]), others, TB * CAP, width), BF),
                pltpu.VMEM((len(chunks[i]), TB + 2, rows, width), BF),
                dma((len(chunks[i]), engines)),
                dma((len(chunks[i]),)),
            ],
            compiler_params=params,
            name="place",
 cost_estimate=TINY,
        )(spread, gates, tails, near_got, *got[i], spread if i == 0 else new_tails)

    new_tails = place(0, None)
    depth = 512
    outs = pl.pallas_call(
        functools.partial(project_body, engines, rows, slots_here, depth),
        grid=(width // depth,),
        in_specs=[pl.BlockSpec((4 * rows, width), lambda i: (0, 0))] * engines
        + [pl.BlockSpec((slots_here, depth, pw), lambda i: (0, i, 0))] * 2
        + [ANY],
        out_specs=[pl.BlockSpec((2 * rows, slots_here * pw), lambda i: (0, 0))] * engines,
        out_shape=[sds((2 * rows, slots_here * pw), BF)] * engines,
        scratch_shapes=[
            pltpu.VMEM((width // depth, 2, engines * 2 * rows, depth), BF),
            pltpu.VMEM((engines * 2 * rows, slots_here * pw), F32),
        ],
        compiler_params=params,
        name="project",
    )(*ys, mr_panels, li_panels, new_tails)

    back = [outs[0]]
    for k, f in rels[1:]:
        back.append(send(outs[2 * ((chips - k) % chips) + f], engines, k, f))
    back[1] = launch(2, back[1])

    per_chan = panel_slot.shape[0] // chans
    blocks_out = pl.pallas_call(
        functools.partial(sort_body, engines, chans, slots_here),
        in_specs=[SM] + [VM] * engines + [ANY] * len(far),
        out_specs=[VM] * chans,
        out_shape=[sds((2 * rows, per_chan * pw), BF)] * chans,
        scratch_shapes=[pltpu.VMEM((engines * slots_here, 2 * rows, pw), BF)],
        compiler_params=params,
        name="sort",
 cost_estimate=TINY,
    )(panel_slot, *back, *got[1])
    total = blocks_out[0].astype(F32)
    for d in range(1, chans):
        total = total + lax.ppermute(blocks_out[d], "chan", [(c, (c + d) % chans) for c in range(chans)]).astype(F32)
    steps_ids = jnp.arange(2, dtype=jnp.int32)
    active = (remaining[None, :] > steps_ids[:, None]).astype(F32)
    total, got[2] = lax.optimization_barrier((total, got[2]))
    mixed = (total.reshape(2, rows, per_chan * pw) * active[:, :, None]).astype(BF)

    new_tails = place(1, new_tails)
    new_tails = place(2, new_tails)
    new_states = pl.pallas_call(
        functools.partial(
            modal_body, engines, rows, [blocks * TB * CAP, len(chunks[state_chunk]) * TB * CAP]
        ),
        in_specs=[SM, ANY, VM, VM] + [ANY] * others,
        out_specs=ANY,
        out_shape=sds((rows, modes, width), F32),
        scratch_shapes=[
            pltpu.VMEM((rows, modes, width), F32),
            pltpu.VMEM((others, CAP * modes, width), BF),
            table,
            tally,
            dma((rows,)),
            dma((others,)),
            dma((rows,)),
        ],
        compiler_params=params,
        name="modal",
 cost_estimate=TINY,
    )(source, modal_states, gates, li_decay, near_got, *got[state_chunk])
    return (mixed, jnp.transpose(new_tails, (1, 0, 2)), new_states)


def solution(mesh):
    return jax.shard_map(
        body,
        mesh=mesh,
        in_specs=(
            P(None, None, ("group", "engine"), "chan"),
            P(None, None, ("group", "engine"), "chan"),
            P(("group", "engine"), None, "chan"),
            P(("group", "engine"), None, "chan"),
            P("group"),
            P(("group", "engine")),
            P(None, "chan"),
            P(None, "chan"),
            P(None, "chan"),
            P("engine", "chan", None),
            P("engine", "chan", None),
            P(),
        ),
        out_specs=(
            P(None, ("group", "engine"), "chan"),
            P(("group", "engine"), None, "chan"),
            P(("group", "engine"), None, "chan"),
        ),
        check_vma=False,
    )
```

```python
import functools

import jax
import jax.numpy as jnp
from jax import lax
from jax.experimental import pallas as pl
from jax.experimental.pallas import tpu as pltpu
from jax.sharding import PartitionSpec as P

CAP = 2
BF = jnp.bfloat16
F32 = jnp.float32
ANY = pl.BlockSpec(memory_space=pl.ANY)
SM = pl.BlockSpec(memory_space=pltpu.SMEM)
VM = pl.BlockSpec(memory_space=pltpu.VMEM)
VLIM = 48 << 20
TB = 16
TINY = pl.CostEstimate(flops=1, transcendentals=0, bytes_accessed=1)


def lane_chunk(width):
    for size in (256, 128):
        if width % size == 0:
            return size
    return width


def wide_chunk(width):
    return 1024 if width % 1024 == 0 else lane_chunk(width)


def links(engines):
    chips = engines // 2
    return [(k, f) for k in range(chips) for f in (0, 1)]


def send(x, engines, k, f):
    chips = engines // 2
    pairs = [(e, ((e // 2 + k) % chips) * 2 + ((e % 2) ^ f)) for e in range(engines)]
    return lax.ppermute(x, "engine", pairs)


def to_engine(me, k, f, engines):
    chips = engines // 2
    return lax.rem(lax.div(me, 2) + k, chips) * 2 + lax.rem(me + f, 2)


def relation_of(me, owner, engines):
    chips = engines // 2
    k = lax.rem(lax.div(me, 2) + chips - lax.div(owner, 2), chips)
    return 2 * k + lax.rem(owner + me, 2)


def departures(engines, rows, source, leave, me):
    for rel, (k, f) in enumerate(links(engines)):
        if rel == 0:
            continue
        there = to_engine(me, k, f, engines)
        for j in range(CAP):
            leave[rel * (CAP + 1) + j] = 0

        found = 0
        for i in range(rows):
            old = source[there * rows + i]
            leave[rel * (CAP + 1) + jnp.minimum(found, CAP)] = lax.rem(old, rows)
            found = found + jnp.where(lax.div(old, rows) == me, 1, 0)


def send_selector(rels, rows, leave, pick):
    height, depth = pick.shape
    at = lax.broadcasted_iota(jnp.int32, (height, 1), 0)
    group = at // (TB * CAP)
    tap = (at % (TB * CAP)) // CAP
    place = at % CAP
    row = jnp.zeros((height, 1), jnp.int32)
    for i, rel in enumerate(rels):
        for j in range(CAP):
            row = jnp.where((group == i) & (place == j), leave[rel * (CAP + 1) + j], row)
    want = tap * rows + row
    pick[...] = (lax.broadcasted_iota(jnp.int32, (height, depth), 1) == want).astype(F32).astype(BF)


def sent_taps(b, tail_len):
    return min(TB, tail_len - 2 - b * TB)


def early_body(engines, rows, blocks, source, tails, *refs):
    far = list(range(2, engines))
    msgs = refs[: len(far)]
    tbuf, pick, leave, tsem = refs[len(far) :]
    tail_len, _, width = tails.shape
    chunk = wide_chunk(width)
    me = lax.axis_index("engine")

    def fetch(n):
        return pltpu.make_async_copy(tails.at[pl.ds(blocks[n] * TB, TB)], tbuf.at[pl.ds(n * TB, TB)], tsem.at[n])

    for n in range(len(blocks)):
        fetch(n).start()
    departures(engines, rows, source, leave, me)
    send_selector(far, rows, leave, pick)
    for n in range(len(blocks)):
        fetch(n).wait()

        for c in range(0, width, chunk):
            cols = pl.ds(c, chunk)
            old = tbuf[n * TB : (n + 1) * TB, :, cols].reshape(TB * rows, chunk)
            rowsel = jnp.dot(pick[...], old, preferred_element_type=F32).astype(BF)
            for i in range(len(far)):
                msgs[i][n * TB * CAP : (n + 1) * TB * CAP, cols] = rowsel[i * TB * CAP : (i + 1) * TB * CAP]


def lead_body(engines, rows, source, tails, states, filt, decay, resid, _, *refs):
    others = engines - 1
    parts = refs[0]
    small = refs[1 : 1 + others]
    fbuf, tbuf, sbuf, leave, tsem, ssem = refs[1 + others :]
    tail_len, _, width = tails.shape
    modes = states.shape[1]
    taps = filt.shape[0]
    chunk = wide_chunk(width)
    me = lax.axis_index("engine")
    total = pl.cdiv(tail_len, TB)

    def fetch(b):
        size = min(TB, tail_len - b * TB)
        return pltpu.make_async_copy(
            tails.at[pl.ds(b * TB, size)], tbuf.at[pl.ds(b * TB, size)], tsem.at[b]
        )

    for b in range(total):
        fetch(b).start()
    load_states = pltpu.make_async_copy(states, sbuf, ssem)
    load_states.start()
    departures(engines, rows, source, leave, me)
    for c in range(0, width, chunk):
        fbuf[0:taps, pl.ds(c, chunk)] = filt[:, pl.ds(c, chunk)].astype(F32)
        fbuf[taps : taps + 8, pl.ds(c, chunk)] = jnp.zeros((8, chunk), F32)
    for b in range(total):
        fetch(b).wait()
        size = min(TB, tail_len - b * TB)

        for c in range(0, width, chunk):
            cols = pl.ds(c, chunk)
            if b == 0:
                first = jnp.zeros((rows, chunk), F32)
                second = jnp.zeros((rows, chunk), F32)
            else:
                first = parts[0, :, cols]
                second = parts[1, :, cols]
            for i in range(size):
                t = tbuf[b * TB + i, :, cols].astype(F32)
                first += t * fbuf[b * TB + i + 1 : b * TB + i + 2, cols]
                second += t * fbuf[b * TB + i + 2 : b * TB + i + 3, cols]
            parts[0, :, cols] = first
            parts[1, :, cols] = second
    load_states.wait()

    def modal(r, carry):
        s = sbuf[r]
        a = resid[...] * (decay[...] * s)
        parts[2, pl.ds(r, 1), :] = jnp.sum(a, axis=0, keepdims=True)
        parts[3, pl.ds(r, 1), :] = jnp.sum(a * decay[...], axis=0, keepdims=True)
        return carry

    lax.fori_loop(0, rows, modal, 0)
    for rel in range(1, engines):
        for j in range(CAP):
            old = leave[rel * (CAP + 1) + j]
            for i in range(4):
                small[rel - 1][4 * j + i : 4 * j + i + 1, :] = parts[i, pl.ds(old, 1), :].astype(BF)
            base = 4 * CAP + j * modes
            small[rel - 1][base : base + modes, :] = sbuf[old].astype(BF)


def pack_body(engines, rows, sends, source, tails, _, *refs):
    far = list(range(2, engines))
    near = refs[0]
    msgs = refs[1 : 1 + len(sends)]
    spread, tbuf, pick, leave, slots, found, tsem = refs[1 + len(msgs) :]
    tail_len, _, width = tails.shape
    chunk = wide_chunk(width)
    me = lax.axis_index("engine")
    total = pl.cdiv(tail_len - 2, TB)
    others = engines - 1

    def fetch(b):
        n = sent_taps(b, tail_len)
        return pltpu.make_async_copy(tails.at[pl.ds(b * TB, n)], tbuf.at[pl.ds(b * TB, n)], tsem.at[b])

    for b in range(total):
        fetch(b).start()
    departures(engines, rows, source, leave, me)
    send_selector([1] + far, rows, leave, pick)
    arrivals(engines, rows, source, slots, found, me)
    height, depth = spread.shape
    at = lax.broadcasted_iota(jnp.int32, (height, 1), 0)
    tap = at // rows
    new_row = at % rows
    want = jnp.zeros((height, 1), jnp.int32)
    for r in range(rows):
        old = source[me * rows + r]
        want = jnp.where(new_row == r, tap * rows + old % rows, want)
    for rel in range(1, engines):
        for j in range(CAP):
            row = jnp.where(found[rel] > j, slots[rel * (CAP + 1) + j], -1)
            want = jnp.where(new_row == row, TB * rows + (rel - 1) * TB * CAP + CAP * tap + j, want)
    spread[...] = (lax.broadcasted_iota(jnp.int32, (height, depth), 1) == want).astype(F32).astype(BF)
    for b in range(total):
        fetch(b).wait()
        n = sent_taps(b, tail_len)
        home = [(msg, rel, blocks) for msg, (rel, blocks) in zip(msgs, sends) if b in blocks]
        tall = pick.shape[0] if home else TB * CAP
        for c in range(0, width, chunk):
            cols = pl.ds(c, chunk)
            old = tbuf[b * TB : b * TB + n, :, cols].reshape(n * rows, chunk)
            rowsel = jnp.dot(pick[0:tall, 0 : n * rows], old, preferred_element_type=F32).astype(BF)
            near[b * TB * CAP : (b + 1) * TB * CAP, cols] = rowsel[0 : TB * CAP]
            for msg, rel, blocks in home:
                base = (b - blocks[0]) * TB * CAP
                msg[base : base + TB * CAP, cols] = rowsel[(rel - 1) * TB * CAP : rel * TB * CAP]


def arrivals(engines, rows, source, slots, found, me):
    for rel in range(engines):
        found[rel] = 0
    for r in range(rows):
        rel = relation_of(me, lax.div(source[me * rows + r], rows), engines)
        at = found[rel]
        slots[rel * (CAP + 1) + jnp.minimum(at, CAP)] = r
        found[rel] = at + 1


def mix_body(engines, rows, source, parts_in, mr, li, filt, decay, resid, *refs):
    got = refs[: engines - 1]
    y, gates, parts, slots, found = refs[-5:]
    width = y.shape[1]
    chunk = lane_chunk(width)
    me = lax.axis_index("engine")
    arrivals(engines, rows, source, slots, found, me)

    def stay(r, carry):
        old = source[me * rows + r] % rows
        for i in range(4):
            parts[i, pl.ds(r, 1), :] = parts_in[i, pl.ds(old, 1), :]
        return carry

    lax.fori_loop(0, rows, stay, 0)
    for rel in range(1, engines):
        for j in range(CAP):

            @pl.when(found[rel] > j)
            def _():
                one = pl.ds(slots[rel * (CAP + 1) + j], 1)
                for i in range(4):
                    parts[i, one, :] = got[rel - 1][4 * j + i : 4 * j + i + 1, :].astype(F32)

    for c in range(0, width, chunk):
        cols = pl.ds(c, chunk)
        f = filt[0:16, cols].astype(F32)
        d = decay[:, cols]
        w = resid[:, cols]
        r0 = jnp.sum(w, axis=0, keepdims=True)
        r1 = jnp.sum(w * d, axis=0, keepdims=True)
        z = []
        for n, qkv in enumerate((mr, mr, li, li)):
            gate = (qkv[n % 2, 1, :, cols].astype(F32) * qkv[n % 2, 2, :, cols].astype(F32)).astype(BF)
            gates[n, :, cols] = gate
            z.append(gate.astype(F32))
        conv0 = f[0:1] * z[0] + parts[0, :, cols]
        conv1 = f[0:1] * z[1] + f[1:2] * z[0] + parts[1, :, cols]
        y[0:rows, cols] = (mr[0, 0, :, cols].astype(F32) * conv0).astype(BF)
        y[rows : 2 * rows, cols] = (mr[1, 0, :, cols].astype(F32) * conv1).astype(BF)
        modal0 = parts[2, :, cols] + z[2] * r0
        modal1 = parts[3, :, cols] + z[2] * r1 + z[3] * r0
        y[2 * rows : 3 * rows, cols] = (li[0, 0, :, cols].astype(F32) * modal0).astype(BF)
        y[3 * rows : 4 * rows, cols] = (li[1, 0, :, cols].astype(F32) * modal1).astype(BF)


def project_body(engines, rows, slots_here, depth, *refs):
    ys = refs[:engines]
    mr_w, li_w = refs[engines : engines + 2]
    outs = refs[-2 - engines : -2]
    x, acc = refs[-2:]
    two = 2 * rows
    width = ys[0].shape[1]
    pw = mr_w.shape[2]
    step = pl.program_id(0)

    @pl.when(step == 0)
    def _():
        for rel in range(engines):
            for b in range(width // depth):
                x[b, 0, rel * two : (rel + 1) * two, :] = ys[rel][0:two, b * depth : (b + 1) * depth]
                x[b, 1, rel * two : (rel + 1) * two, :] = ys[rel][two : 2 * two, b * depth : (b + 1) * depth]
        acc[...] = jnp.zeros_like(acc)

    for g in range(slots_here):
        cols = slice(g * pw, (g + 1) * pw)
        acc[:, cols] += jnp.dot(x[step, 0], mr_w[g], preferred_element_type=F32) + jnp.dot(
            x[step, 1], li_w[g], preferred_element_type=F32
        )

    @pl.when(step == pl.num_programs(0) - 1)
    def _():
        for rel in range(engines):
            outs[rel][...] = acc[rel * two : (rel + 1) * two, :].astype(BF)


def sort_body(engines, chans, slots_here, slot_of, *refs):
    got = refs[:engines]
    outs = refs[-1 - chans : -1]
    tiles = refs[-1]
    pw = tiles.shape[2]
    me = lax.axis_index("engine")
    here = lax.axis_index("chan")
    per_chan = slot_of.shape[0] // chans
    for rel in range(engines):
        for g in range(slots_here):
            tiles[rel * slots_here + g] = got[rel][:, g * pw : (g + 1) * pw]
    for d in range(chans):
        there = (here + d) % chans
        for h in range(per_chan):
            slot = slot_of[there * per_chan + h]
            rel = relation_of(me, slot // slots_here, engines)
            outs[d][:, h * pw : (h + 1) * pw] = tiles[rel * slots_here + slot % slots_here]


def place_body(engines, rows, blocks, kept, layout, spread, gates, tails, near, *refs):
    msgs = refs[: len(layout)]
    if kept:
        new, tbuf, isem = refs[len(layout) :]
    else:
        new, tbuf, obuf, isem, osem = refs[len(layout) + 1 :]
    tail_len, _, width = tails.shape
    chunk = wide_chunk(width)
    lead = 2 if blocks[0] == 0 else 0

    def fetch(n):
        b = blocks[n]
        taps = sent_taps(b, tail_len)
        return pltpu.make_async_copy(tails.at[pl.ds(b * TB, taps)], tbuf.at[n, pl.ds(0, taps)], isem.at[n])

    def store(n):
        b = blocks[n]
        taps = sent_taps(b, tail_len)
        extra = lead if n == 0 else 0
        return pltpu.make_async_copy(
            obuf.at[n, pl.ds(2 - extra, taps + extra)], new.at[pl.ds(b * TB + 2 - extra, taps + extra)], osem.at[n]
        )

    for n in range(len(blocks)):
        fetch(n).start()
    if lead:
        obuf[0, 0] = gates[1]
        obuf[0, 1] = gates[0]
    for n, b in enumerate(blocks):
        fetch(n).wait()
        taps = sent_taps(b, tail_len)
        top = taps * rows
        for c in range(0, width, chunk):
            cols = pl.ds(c, chunk)
            old = tbuf[n, 0:taps, :, cols].reshape(top, chunk)
            got = [near[b * TB * CAP : (b + 1) * TB * CAP, cols]]
            for msg, held in zip(msgs, layout):
                if b in held:
                    got.append(msg[(b - held[0]) * TB * CAP : (b - held[0] + 1) * TB * CAP, cols])
            got = jnp.concatenate(got, axis=0)
            rest = TB * rows + got.shape[0]
            value = jnp.dot(spread[0:top, 0:top], old, preferred_element_type=F32) + jnp.dot(
                spread[0:top, TB * rows : rest], got, preferred_element_type=F32
            )
            value = value.astype(BF).reshape(taps, rows, chunk)
            if kept:
                new[n, 0:taps, :, cols] = value
            else:
                obuf[n, 2 : 2 + taps, :, cols] = value
        if not kept:
            store(n).start()
    if not kept:
        for n in range(len(blocks)):
            store(n).wait()


def last_body(engines, rows, blocks, spread, base, msg, _, new_tails, obuf, osem):
    tail_len, _, width = new_tails.shape
    chunk = wide_chunk(width)

    def store(n):
        b = blocks[n]
        taps = sent_taps(b, tail_len)
        return pltpu.make_async_copy(obuf.at[n, pl.ds(0, taps)], new_tails.at[pl.ds(b * TB + 2, taps)], osem.at[n])

    left = spread.shape[1] - TB * CAP
    for n, b in enumerate(blocks):
        taps = sent_taps(b, tail_len)
        top = taps * rows
        for c in range(0, width, chunk):
            cols = pl.ds(c, chunk)
            value = jnp.dot(
                spread[0:top, left:], msg[n * TB * CAP : (n + 1) * TB * CAP, cols], preferred_element_type=F32
            )
            value = value + base[n, 0:taps, :, cols].reshape(top, chunk).astype(F32)
            obuf[n, 0:taps, :, cols] = value.astype(BF).reshape(taps, rows, chunk)
        store(n).start()
    for n in range(len(blocks)):
        store(n).wait()


def modal_body(engines, rows, source, states, gates, decay, *refs):
    others = engines - 1
    msgs = refs[:others]
    new_states = refs[others]
    sbuf, z, slots, found, isem, osem = refs[others + 1 :]
    modes = states.shape[1]
    me = lax.axis_index("engine")

    def fetch(r):
        return pltpu.make_async_copy(states.at[lax.rem(source[me * rows + r], rows)], sbuf.at[r], isem.at[r])

    def store(r):
        return pltpu.make_async_copy(sbuf.at[r], new_states.at[r], osem.at[r])

    def stays(r):
        return lax.div(source[me * rows + r], rows) == me

    def begin(r, carry):
        @pl.when(stays(r))
        def _():
            fetch(r).start()

        return carry

    lax.fori_loop(0, rows, begin, 0)
    z[...] = gates[2:4].astype(F32)
    arrivals(engines, rows, source, slots, found, me)

    def advance(r, s):
        d = decay[...]
        sbuf[r] = d * (d * s + z[0, pl.ds(r, 1), :]) + z[1, pl.ds(r, 1), :]
        store(r).start()

    for rel in range(1, engines):
        for j in range(CAP):

            @pl.when(found[rel] > j)
            def _():
                base = 4 * CAP + j * modes
                advance(slots[rel * (CAP + 1) + j], msgs[rel - 1][base : base + modes, :].astype(F32))

    def work(r, carry):
        @pl.when(stays(r))
        def _():
            fetch(r).wait()
            advance(r, sbuf[r])

        return carry

    lax.fori_loop(0, rows, work, 0)

    def finish(r, carry):
        store(r).wait()
        return carry

    lax.fori_loop(0, rows, finish, 0)


def split(total):
    cuts = [0, 2 * total // 8, 5 * total // 8, total]
    return [list(range(a, b)) for a, b in zip(cuts, cuts[1:]) if a < b]


def body(mr_qkv, li_qkv, conv_tails, modal_states, source, remaining, mr_filter, li_decay, li_residue, mr_panels,
         li_panels, panel_slot):
    engines = lax.axis_size("engine")
    chans = lax.axis_size("chan")
    rows, tail_len, width = conv_tails.shape
    modes = modal_states.shape[1]
    taps = mr_filter.shape[0]
    slots_here, _, pw = mr_panels.shape
    others = engines - 1
    chips = engines // 2
    rels = links(engines)
    far = list(range(2, engines))
    sds = jax.ShapeDtypeStruct
    dma = pltpu.SemaphoreType.DMA
    params = pltpu.CompilerParams(vmem_limit_bytes=VLIM)
    tails = jnp.transpose(conv_tails, (1, 0, 2))
    blocks = pl.cdiv(tail_len - 2, TB)
    chunks = split(blocks)
    table = pltpu.SMEM((engines * (CAP + 1),), jnp.int32)
    tally = pltpu.SMEM((engines,), jnp.int32)

    def msg_rows(i):
        return len(chunks[i]) * TB * CAP

    msgs = {}
    msgs[0] = pl.pallas_call(
        functools.partial(early_body, engines, rows, chunks[0]),
        in_specs=[SM, ANY],
        out_specs=[VM] * len(far),
        out_shape=[sds((msg_rows(0), width), BF)] * len(far),
        scratch_shapes=[
            pltpu.VMEM((len(chunks[0]) * TB, rows, width), BF),
            pltpu.VMEM((len(far) * TB * CAP, TB * rows), BF),
            table,
            dma((len(chunks[0]),)),
        ],
        compiler_params=params,
        name="early",
    )(source, tails)
    got = {}

    def launch(i, token=None):
        arrays = list(msgs[i])
        if token is not None:
            arrays, token = lax.optimization_barrier((arrays, token))
        got[i] = [send(a, engines, *rels[rel]) for a, rel in zip(arrays, far)]
        return token

    launch(0)
    lead = pl.pallas_call(
        functools.partial(lead_body, engines, rows),
        in_specs=[SM, ANY, ANY, VM, VM, VM, ANY],
        out_specs=[VM] * (1 + others),
        out_shape=[sds((4, rows, width), F32)] + [sds((CAP * (4 + modes), width), BF)] * others,
        scratch_shapes=[
            pltpu.VMEM((taps + 8, width), F32),
            pltpu.VMEM((tail_len, rows, width), BF),
            pltpu.VMEM((rows, modes, width), F32),
            table,
            dma((pl.cdiv(tail_len, TB),)),
            dma(()),
        ],
        compiler_params=params,
        name="lead",
    )(source, tails, modal_states, mr_filter, li_decay, li_residue, msgs[0][0])
    parts = lead[0]
    small = lead[1 : 1 + others]
    parts_got = [send(small[rel - 1], engines, *rels[rel]) for rel in range(1, engines)]

    sends = []
    for i in range(1, len(chunks)):
        sends += [(rel, chunks[i]) for rel in far]
    packed = pl.pallas_call(
        functools.partial(pack_body, engines, rows, sends),
        in_specs=[SM, ANY, ANY],
        out_specs=[VM] * (2 + len(sends)),
        out_shape=[sds((blocks * TB * CAP, width), BF)]
        + [sds((len(group) * TB * CAP, width), BF) for _, group in sends]
        + [sds((TB * rows, TB * rows + others * TB * CAP), BF)],
        scratch_shapes=[
            pltpu.VMEM((tail_len, rows, width), BF),
            pltpu.VMEM((others * TB * CAP, TB * rows), BF),
            table,
            table,
            tally,
            dma((blocks,)),
        ],
        compiler_params=params,
        name="pack",
    )(source, tails, small[0])
    near_msg = packed[0]
    spread = packed[-1]
    msgs[1] = packed[1 : 1 + len(far)]
    msgs[2] = packed[1 + len(far) : 1 + 2 * len(far)]

    y, gates = pl.pallas_call(
        functools.partial(mix_body, engines, rows),
        in_specs=[SM] + [VM] * (6 + others) + [ANY] * (1 + len(far)),
        out_specs=[VM, VM],
        out_shape=[sds((4 * rows, width), BF), sds((4, rows, width), BF)],
        scratch_shapes=[pltpu.VMEM((4, rows, width), F32), table, tally],
        compiler_params=params,
        name="mix",
    )(source, parts, mr_qkv, li_qkv, mr_filter, li_decay, li_residue, *parts_got, spread, *got[0])

    near_msg, y = lax.optimization_barrier((near_msg, y))
    near_got = send(near_msg, engines, 0, 1)
    same_core = [y] + [send(y, engines, k, 0) for k in range(1, chips)]
    ys = []
    for k in range(chips):
        ys += [same_core[k], send(same_core[k], engines, 0, 1)]
    ys[1] = launch(1, ys[1])

    def place(i, arrays, layout, tails_so_far, kept=False):
        group = chunks[i]
        buffer = pltpu.VMEM((len(group), TB, rows, width), BF)
        carry = [] if kept else [gates if tails_so_far is None else tails_so_far]
        return pl.pallas_call(
            functools.partial(place_body, engines, rows, group, kept, layout),
            in_specs=[VM, VM, ANY] + [VM] * (1 + len(arrays)) + [ANY] * len(carry),
            out_specs=VM if kept else ANY,
            out_shape=sds(buffer.shape if kept else (tail_len, rows, width), BF),
            input_output_aliases={} if tails_so_far is None else {4 + len(arrays): 0},
            scratch_shapes=[buffer, dma((len(group),))]
            if kept
            else [buffer, pltpu.VMEM((len(group), TB + 2, rows, width), BF), dma((len(group),)), dma((len(group),))],
            compiler_params=params,
            name="place",
            cost_estimate=TINY,
        )(spread, gates, tails, near_got, *arrays, *carry)

    new_tails = place(0, got[0], [chunks[0]] * len(far), None)
    depth = 512
    outs = pl.pallas_call(
        functools.partial(project_body, engines, rows, slots_here, depth),
        grid=(width // depth,),
        in_specs=[pl.BlockSpec((4 * rows, width), lambda i: (0, 0))] * engines
        + [pl.BlockSpec((slots_here, depth, pw), lambda i: (0, i, 0))] * 2
        + [ANY],
        out_specs=[pl.BlockSpec((2 * rows, slots_here * pw), lambda i: (0, 0))] * engines,
        out_shape=[sds((2 * rows, slots_here * pw), BF)] * engines,
        scratch_shapes=[
            pltpu.VMEM((width // depth, 2, engines * 2 * rows, depth), BF),
            pltpu.VMEM((engines * 2 * rows, slots_here * pw), F32),
        ],
        compiler_params=params,
        name="project",
    )(*ys, mr_panels, li_panels, new_tails)

    back = [outs[0]]
    for k, f in rels[1:]:
        back.append(send(outs[2 * ((chips - k) % chips) + f], engines, k, f))
    got[1] = launch(2, got[1])

    new_states = pl.pallas_call(
        functools.partial(modal_body, engines, rows),
        in_specs=[SM, ANY, VM, VM] + [VM] * others,
        out_specs=ANY,
        out_shape=sds((rows, modes, width), F32),
        scratch_shapes=[
            pltpu.VMEM((rows, modes, width), F32),
            pltpu.VMEM((2, rows, width), F32),
            table,
            tally,
            dma((rows,)),
            dma((rows,)),
        ],
        compiler_params=params,
        name="modal",
        cost_estimate=TINY,
    )(source, modal_states, gates, li_decay, *parts_got)

    back[1], new_states = lax.optimization_barrier((back[1], new_states))
    per_chan = panel_slot.shape[0] // chans
    blocks_out = pl.pallas_call(
        functools.partial(sort_body, engines, chans, slots_here),
        in_specs=[SM] + [VM] * engines + [ANY] * len(far),
        out_specs=[VM] * chans,
        out_shape=[sds((2 * rows, per_chan * pw), BF)] * chans,
        scratch_shapes=[pltpu.VMEM((engines * slots_here, 2 * rows, pw), BF)],
        compiler_params=params,
        name="sort",
        cost_estimate=TINY,
    )(panel_slot, *back, *got[1])
    total = blocks_out[0].astype(F32)
    for d in range(1, chans):
        total = total + lax.ppermute(blocks_out[d], "chan", [(c, (c + d) % chans) for c in range(chans)]).astype(F32)
    steps_ids = jnp.arange(2, dtype=jnp.int32)
    active = (remaining[None, :] > steps_ids[:, None]).astype(F32)
    total, got[2][0] = lax.optimization_barrier((total, got[2][0]))
    mixed = (total.reshape(2, rows, per_chan * pw) * active[:, :, None]).astype(BF)

    new_tails = place(1, got[1], [chunks[1]] * len(far), new_tails)
    base = place(2, got[2][:-1], [chunks[2]] * (len(far) - 1), None, True)
    buffer = pltpu.VMEM((len(chunks[2]), TB, rows, width), BF)
    new_tails = pl.pallas_call(
        functools.partial(last_body, engines, rows, chunks[2]),
        in_specs=[VM, VM, VM, ANY],
        out_specs=ANY,
        out_shape=sds((tail_len, rows, width), BF),
        input_output_aliases={3: 0},
        scratch_shapes=[buffer, dma((len(chunks[2]),))],
        compiler_params=params,
        name="last",
        cost_estimate=TINY,
    )(spread, base, got[2][-1], new_tails)
    return (mixed, jnp.transpose(new_tails, (1, 0, 2)), new_states)


def solution(mesh):
    return jax.shard_map(
        body,
        mesh=mesh,
        in_specs=(
            P(None, None, ("group", "engine"), "chan"),
            P(None, None, ("group", "engine"), "chan"),
            P(("group", "engine"), None, "chan"),
            P(("group", "engine"), None, "chan"),
            P("group"),
            P(("group", "engine")),
            P(None, "chan"),
            P(None, "chan"),
            P(None, "chan"),
            P("engine", "chan", None),
            P("engine", "chan", None),
            P(),
        ),
        out_specs=(
            P(None, ("group", "engine"), "chan"),
            P(("group", "engine"), None, "chan"),
            P(("group", "engine"), None, "chan"),
        ),
        check_vma=False,
    )
```

```python
import functools

import jax
import jax.numpy as jnp
from jax import lax
from jax.experimental import pallas as pl
from jax.experimental.pallas import tpu as pltpu
from jax.sharding import PartitionSpec as P

CAP = 2
BF = jnp.bfloat16
F32 = jnp.float32
ANY = pl.BlockSpec(memory_space=pl.ANY)
SM = pl.BlockSpec(memory_space=pltpu.SMEM)
VM = pl.BlockSpec(memory_space=pltpu.VMEM)
VLIM = 48 << 20
TB = 16
TINY = pl.CostEstimate(flops=1, transcendentals=0, bytes_accessed=1)


def lane_chunk(width):
    for size in (256, 128):
        if width % size == 0:
            return size
    return width


def wide_chunk(width):
    return 1024 if width % 1024 == 0 else lane_chunk(width)


def links(engines):
    chips = engines // 2
    return [(k, f) for k in range(chips) for f in (0, 1)]


def send(x, engines, k, f):
    chips = engines // 2
    pairs = [(e, ((e // 2 + k) % chips) * 2 + ((e % 2) ^ f)) for e in range(engines)]
    return lax.ppermute(x, "engine", pairs)


def to_engine(me, k, f, engines):
    chips = engines // 2
    return lax.rem(lax.div(me, 2) + k, chips) * 2 + lax.rem(me + f, 2)


def relation_of(me, owner, engines):
    chips = engines // 2
    k = lax.rem(lax.div(me, 2) + chips - lax.div(owner, 2), chips)
    return 2 * k + lax.rem(owner + me, 2)


def departures(engines, rows, source, leave, me):
    for rel, (k, f) in enumerate(links(engines)):
        if rel == 0:
            continue
        there = to_engine(me, k, f, engines)
        for j in range(CAP):
            leave[rel * (CAP + 1) + j] = 0

        found = 0
        for i in range(rows):
            old = source[there * rows + i]
            leave[rel * (CAP + 1) + jnp.minimum(found, CAP)] = lax.rem(old, rows)
            found = found + jnp.where(lax.div(old, rows) == me, 1, 0)


def send_selector(rels, rows, leave, pick):
    height, depth = pick.shape
    at = lax.broadcasted_iota(jnp.int32, (height, 1), 0)
    group = at // (TB * CAP)
    tap = (at % (TB * CAP)) // CAP
    place = at % CAP
    row = jnp.zeros((height, 1), jnp.int32)
    for i, rel in enumerate(rels):
        for j in range(CAP):
            row = jnp.where((group == i) & (place == j), leave[rel * (CAP + 1) + j], row)
    want = tap * rows + row
    pick[...] = (lax.broadcasted_iota(jnp.int32, (height, depth), 1) == want).astype(F32).astype(BF)


def sent_taps(b, tail_len):
    return min(TB, tail_len - 2 - b * TB)


def early_body(engines, rows, blocks, source_far, tails, *refs):
    far = list(range(2, engines))
    msgs = refs[: len(far)]
    source, tbuf, pick, leave, tsem, source_sem = refs[len(far) :]
    tail_len, _, width = tails.shape
    chunk = wide_chunk(width)
    me = lax.axis_index("engine")

    def fetch(n):
        return pltpu.make_async_copy(tails.at[pl.ds(blocks[n] * TB, TB)], tbuf.at[pl.ds(n * TB, TB)], tsem.at[n])

    read = pltpu.make_async_copy(source_far, source, source_sem)
    read.start()
    for n in range(len(blocks)):
        fetch(n).start()
    read.wait()
    departures(engines, rows, source, leave, me)
    send_selector(far, rows, leave, pick)
    for n in range(len(blocks)):
        fetch(n).wait()

        for c in range(0, width, chunk):
            cols = pl.ds(c, chunk)
            old = tbuf[n * TB : (n + 1) * TB, :, cols].reshape(TB * rows, chunk)
            rowsel = jnp.dot(pick[...], old, preferred_element_type=F32).astype(BF)
            for i in range(len(far)):
                msgs[i][n * TB * CAP : (n + 1) * TB * CAP, cols] = rowsel[i * TB * CAP : (i + 1) * TB * CAP]


def lead_body(engines, rows, source, tails, states, filt, decay, resid, _, *refs):
    others = engines - 1
    parts = refs[0]
    small = refs[1 : 1 + others]
    fbuf, tbuf, sbuf, leave, tsem, ssem = refs[1 + others :]
    tail_len, _, width = tails.shape
    modes = states.shape[1]
    taps = filt.shape[0]
    chunk = wide_chunk(width)
    me = lax.axis_index("engine")
    total = pl.cdiv(tail_len, TB)

    def fetch(b):
        size = min(TB, tail_len - b * TB)
        return pltpu.make_async_copy(
            tails.at[pl.ds(b * TB, size)], tbuf.at[pl.ds(b * TB, size)], tsem.at[b]
        )

    for b in range(total):
        fetch(b).start()
    load_states = pltpu.make_async_copy(states, sbuf, ssem)
    load_states.start()
    departures(engines, rows, source, leave, me)
    for c in range(0, width, chunk):
        fbuf[0:taps, pl.ds(c, chunk)] = filt[:, pl.ds(c, chunk)].astype(F32)
        fbuf[taps : taps + 8, pl.ds(c, chunk)] = jnp.zeros((8, chunk), F32)
    for b in range(total):
        fetch(b).wait()
        size = min(TB, tail_len - b * TB)

        for c in range(0, width, chunk):
            cols = pl.ds(c, chunk)
            if b == 0:
                first = jnp.zeros((rows, chunk), F32)
                second = jnp.zeros((rows, chunk), F32)
            else:
                first = parts[0, :, cols]
                second = parts[1, :, cols]
            for i in range(size):
                t = tbuf[b * TB + i, :, cols].astype(F32)
                first += t * fbuf[b * TB + i + 1 : b * TB + i + 2, cols]
                second += t * fbuf[b * TB + i + 2 : b * TB + i + 3, cols]
            parts[0, :, cols] = first
            parts[1, :, cols] = second
    load_states.wait()

    def modal(r, carry):
        s = sbuf[r]
        a = resid[...] * (decay[...] * s)
        parts[2, pl.ds(r, 1), :] = jnp.sum(a, axis=0, keepdims=True)
        parts[3, pl.ds(r, 1), :] = jnp.sum(a * decay[...], axis=0, keepdims=True)
        return carry

    lax.fori_loop(0, rows, modal, 0)
    for rel in range(1, engines):
        for j in range(CAP):
            old = leave[rel * (CAP + 1) + j]
            for i in range(4):
                small[rel - 1][4 * j + i : 4 * j + i + 1, :] = parts[i, pl.ds(old, 1), :].astype(BF)
            base = 4 * CAP + j * modes
            small[rel - 1][base : base + modes, :] = sbuf[old].astype(BF)


def pack_body(engines, rows, sends, source, tails, parts_in, *refs):
    far = list(range(2, engines))
    near = refs[0]
    msgs = refs[1 : 1 + len(sends)]
    spread, parts, tbuf, pick, leave, slots, found, tsem = refs[1 + len(msgs) :]
    tail_len, _, width = tails.shape
    chunk = wide_chunk(width)
    me = lax.axis_index("engine")
    total = pl.cdiv(tail_len - 2, TB)
    others = engines - 1

    def fetch(b):
        n = sent_taps(b, tail_len)
        return pltpu.make_async_copy(tails.at[pl.ds(b * TB, n)], tbuf.at[pl.ds(b * TB, n)], tsem.at[b])

    for b in range(total):
        fetch(b).start()
    departures(engines, rows, source, leave, me)
    send_selector([1] + far, rows, leave, pick)
    arrivals(engines, rows, source, slots, found, me)
    height, depth = spread.shape
    at = lax.broadcasted_iota(jnp.int32, (height, 1), 0)
    tap = at // rows
    new_row = at % rows
    want = jnp.zeros((height, 1), jnp.int32)
    for r in range(rows):
        old = source[me * rows + r]
        want = jnp.where(new_row == r, tap * rows + old % rows, want)
    for rel in range(1, engines):
        for j in range(CAP):
            row = jnp.where(found[rel] > j, slots[rel * (CAP + 1) + j], -1)
            want = jnp.where(new_row == row, TB * rows + (rel - 1) * TB * CAP + CAP * tap + j, want)
    spread[...] = (lax.broadcasted_iota(jnp.int32, (height, depth), 1) == want).astype(F32).astype(BF)

    def stay(r, carry):
        old = lax.rem(source[me * rows + r], rows)
        for i in range(4):
            parts[i, pl.ds(r, 1), :] = parts_in[i, pl.ds(old, 1), :]
        return carry

    lax.fori_loop(0, rows, stay, 0)
    for b in range(total):
        fetch(b).wait()
        n = sent_taps(b, tail_len)
        home = [(msg, rel, blocks) for msg, (rel, blocks) in zip(msgs, sends) if b in blocks]
        tall = pick.shape[0] if home else TB * CAP
        for c in range(0, width, chunk):
            cols = pl.ds(c, chunk)
            old = tbuf[b * TB : b * TB + n, :, cols].reshape(n * rows, chunk)
            rowsel = jnp.dot(pick[0:tall, 0 : n * rows], old, preferred_element_type=F32).astype(BF)
            near[b * TB * CAP : (b + 1) * TB * CAP, cols] = rowsel[0 : TB * CAP]
            for msg, rel, blocks in home:
                base = (b - blocks[0]) * TB * CAP
                msg[base : base + TB * CAP, cols] = rowsel[(rel - 1) * TB * CAP : rel * TB * CAP]


def arrivals(engines, rows, source, slots, found, me):
    for rel in range(engines):
        found[rel] = 0
    for r in range(rows):
        rel = relation_of(me, lax.div(source[me * rows + r], rows), engines)
        at = found[rel]
        slots[rel * (CAP + 1) + jnp.minimum(at, CAP)] = r
        found[rel] = at + 1


def mix_body(engines, rows, source, parts_in, mr, li, filt, decay, resid, *refs):
    got = refs[: engines - 1]
    y, gates, parts, slots, found = refs[-5:]
    width = y.shape[1]
    chunk = lane_chunk(width)
    me = lax.axis_index("engine")
    arrivals(engines, rows, source, slots, found, me)

    parts[...] = parts_in[...]
    for rel in range(1, engines):
        for j in range(CAP):

            @pl.when(found[rel] > j)
            def _():
                one = pl.ds(slots[rel * (CAP + 1) + j], 1)
                for i in range(4):
                    parts[i, one, :] = got[rel - 1][4 * j + i : 4 * j + i + 1, :].astype(F32)

    for c in range(0, width, chunk):
        cols = pl.ds(c, chunk)
        f = filt[0:16, cols].astype(F32)
        d = decay[:, cols]
        w = resid[:, cols]
        r0 = jnp.sum(w, axis=0, keepdims=True)
        r1 = jnp.sum(w * d, axis=0, keepdims=True)
        z = []
        for n, qkv in enumerate((mr, mr, li, li)):
            gate = (qkv[n % 2, 1, :, cols].astype(F32) * qkv[n % 2, 2, :, cols].astype(F32)).astype(BF)
            gates[n, :, cols] = gate
            z.append(gate.astype(F32))
        conv0 = f[0:1] * z[0] + parts[0, :, cols]
        conv1 = f[0:1] * z[1] + f[1:2] * z[0] + parts[1, :, cols]
        y[0:rows, cols] = (mr[0, 0, :, cols].astype(F32) * conv0).astype(BF)
        y[rows : 2 * rows, cols] = (mr[1, 0, :, cols].astype(F32) * conv1).astype(BF)
        modal0 = parts[2, :, cols] + z[2] * r0
        modal1 = parts[3, :, cols] + z[2] * r1 + z[3] * r0
        y[2 * rows : 3 * rows, cols] = (li[0, 0, :, cols].astype(F32) * modal0).astype(BF)
        y[3 * rows : 4 * rows, cols] = (li[1, 0, :, cols].astype(F32) * modal1).astype(BF)


def project_body(engines, rows, slots_here, depth, *refs):
    ys = refs[:engines]
    mr_w, li_w = refs[engines : engines + 2]
    outs = refs[-2 - engines : -2]
    x, acc = refs[-2:]
    two = 2 * rows
    width = ys[0].shape[1]
    pw = mr_w.shape[2]
    step = pl.program_id(0)

    @pl.when(step == 0)
    def _():
        for rel in range(engines):
            for b in range(width // depth):
                x[b, 0, rel * two : (rel + 1) * two, :] = ys[rel][0:two, b * depth : (b + 1) * depth]
                x[b, 1, rel * two : (rel + 1) * two, :] = ys[rel][two : 2 * two, b * depth : (b + 1) * depth]
        acc[...] = jnp.zeros_like(acc)

    for g in range(slots_here):
        cols = slice(g * pw, (g + 1) * pw)
        acc[:, cols] += jnp.dot(x[step, 0], mr_w[g], preferred_element_type=F32) + jnp.dot(
            x[step, 1], li_w[g], preferred_element_type=F32
        )

    @pl.when(step == pl.num_programs(0) - 1)
    def _():
        for rel in range(engines):
            outs[rel][...] = acc[rel * two : (rel + 1) * two, :].astype(BF)


def sort_body(engines, chans, slots_here, slot_of, *refs):
    got = refs[:engines]
    outs = refs[-1 - chans : -1]
    tiles = refs[-1]
    pw = tiles.shape[2]
    me = lax.axis_index("engine")
    here = lax.axis_index("chan")
    per_chan = slot_of.shape[0] // chans
    for rel in range(engines):
        for g in range(slots_here):
            tiles[rel * slots_here + g] = got[rel][:, g * pw : (g + 1) * pw]
    for d in range(chans):
        there = (here + d) % chans
        for h in range(per_chan):
            slot = slot_of[there * per_chan + h]
            rel = relation_of(me, slot // slots_here, engines)
            outs[d][:, h * pw : (h + 1) * pw] = tiles[rel * slots_here + slot % slots_here]


def place_body(engines, rows, blocks, kept, layout, spread, gates, tails, near, *refs):
    msgs = refs[: len(layout)]
    if kept:
        new, tbuf, isem = refs[len(layout) :]
    else:
        new, tbuf, obuf, isem, osem = refs[len(layout) + 1 :]
    tail_len, _, width = tails.shape
    chunk = wide_chunk(width)
    lead = 2 if blocks[0] == 0 else 0

    def fetch(n):
        b = blocks[n]
        taps = sent_taps(b, tail_len)
        return pltpu.make_async_copy(tails.at[pl.ds(b * TB, taps)], tbuf.at[n, pl.ds(0, taps)], isem.at[n])

    def store(n):
        b = blocks[n]
        taps = sent_taps(b, tail_len)
        extra = lead if n == 0 else 0
        return pltpu.make_async_copy(
            obuf.at[n, pl.ds(2 - extra, taps + extra)], new.at[pl.ds(b * TB + 2 - extra, taps + extra)], osem.at[n]
        )

    for n in range(len(blocks)):
        fetch(n).start()
    if lead:
        obuf[0, 0] = gates[1]
        obuf[0, 1] = gates[0]
    for n, b in enumerate(blocks):
        fetch(n).wait()
        taps = sent_taps(b, tail_len)
        top = taps * rows
        for c in range(0, width, chunk):
            cols = pl.ds(c, chunk)
            old = tbuf[n, 0:taps, :, cols].reshape(top, chunk)
            got = [near[b * TB * CAP : (b + 1) * TB * CAP, cols]]
            for msg, held in zip(msgs, layout):
                if b in held:
                    got.append(msg[(b - held[0]) * TB * CAP : (b - held[0] + 1) * TB * CAP, cols])
            got = jnp.concatenate(got, axis=0)
            rest = TB * rows + got.shape[0]
            value = jnp.dot(spread[0:top, 0:top], old, preferred_element_type=F32) + jnp.dot(
                spread[0:top, TB * rows : rest], got, preferred_element_type=F32
            )
            value = value.astype(BF).reshape(taps, rows, chunk)
            if kept:
                new[n, 0:taps, :, cols] = value
            else:
                obuf[n, 2 : 2 + taps, :, cols] = value
        if not kept:
            store(n).start()
    if not kept:
        for n in range(len(blocks)):
            store(n).wait()


def last_body(engines, rows, blocks, spread, base, msg, _, new_tails, obuf, osem):
    tail_len, _, width = new_tails.shape
    chunk = wide_chunk(width)

    def store(n):
        b = blocks[n]
        taps = sent_taps(b, tail_len)
        return pltpu.make_async_copy(obuf.at[n, pl.ds(0, taps)], new_tails.at[pl.ds(b * TB + 2, taps)], osem.at[n])

    left = spread.shape[1] - TB * CAP
    for n, b in enumerate(blocks):
        taps = sent_taps(b, tail_len)
        top = taps * rows
        for c in range(0, width, chunk):
            cols = pl.ds(c, chunk)
            value = jnp.dot(
                spread[0:top, left:], msg[n * TB * CAP : (n + 1) * TB * CAP, cols], preferred_element_type=F32
            )
            value = value + base[n, 0:taps, :, cols].reshape(top, chunk).astype(F32)
            obuf[n, 0:taps, :, cols] = value.astype(BF).reshape(taps, rows, chunk)
        store(n).start()
    for n in range(len(blocks)):
        store(n).wait()


def modal_body(engines, rows, source, states, gates, decay, *refs):
    others = engines - 1
    msgs = refs[:others]
    new_states = refs[others]
    sbuf, z, slots, found, isem, osem = refs[others + 1 :]
    modes = states.shape[1]
    me = lax.axis_index("engine")

    def fetch(r):
        return pltpu.make_async_copy(states.at[lax.rem(source[me * rows + r], rows)], sbuf.at[r], isem.at[r])

    def store(r):
        return pltpu.make_async_copy(sbuf.at[r], new_states.at[r], osem.at[r])

    def stays(r):
        return lax.div(source[me * rows + r], rows) == me

    def begin(r, carry):
        @pl.when(stays(r))
        def _():
            fetch(r).start()

        return carry

    lax.fori_loop(0, rows, begin, 0)
    z[...] = gates[2:4].astype(F32)
    arrivals(engines, rows, source, slots, found, me)

    def advance(r, s):
        d = decay[...]
        sbuf[r] = d * (d * s + z[0, pl.ds(r, 1), :]) + z[1, pl.ds(r, 1), :]
        store(r).start()

    for rel in range(1, engines):
        for j in range(CAP):

            @pl.when(found[rel] > j)
            def _():
                base = 4 * CAP + j * modes
                advance(slots[rel * (CAP + 1) + j], msgs[rel - 1][base : base + modes, :].astype(F32))

    def work(r, carry):
        @pl.when(stays(r))
        def _():
            fetch(r).wait()
            advance(r, sbuf[r])

        return carry

    lax.fori_loop(0, rows, work, 0)

    def finish(r, carry):
        store(r).wait()
        return carry

    lax.fori_loop(0, rows, finish, 0)


def split(total):
    cuts = [0, 2 * total // 8, 5 * total // 8, total]
    return [list(range(a, b)) for a, b in zip(cuts, cuts[1:]) if a < b]


def body(mr_qkv, li_qkv, conv_tails, modal_states, source, remaining, mr_filter, li_decay, li_residue, mr_panels,
         li_panels, panel_slot):
    engines = lax.axis_size("engine")
    chans = lax.axis_size("chan")
    rows, tail_len, width = conv_tails.shape
    modes = modal_states.shape[1]
    taps = mr_filter.shape[0]
    slots_here, _, pw = mr_panels.shape
    others = engines - 1
    chips = engines // 2
    rels = links(engines)
    far = list(range(2, engines))
    sds = jax.ShapeDtypeStruct
    dma = pltpu.SemaphoreType.DMA
    params = pltpu.CompilerParams(vmem_limit_bytes=VLIM)
    tails = jnp.transpose(conv_tails, (1, 0, 2))
    blocks = pl.cdiv(tail_len - 2, TB)
    chunks = split(blocks)
    table = pltpu.SMEM((engines * (CAP + 1),), jnp.int32)
    tally = pltpu.SMEM((engines,), jnp.int32)

    def msg_rows(i):
        return len(chunks[i]) * TB * CAP

    msgs = {}
    msgs[0] = pl.pallas_call(
        functools.partial(early_body, engines, rows, chunks[0]),
        in_specs=[ANY, ANY],
        out_specs=[VM] * len(far),
        out_shape=[sds((msg_rows(0), width), BF)] * len(far),
        scratch_shapes=[
            pltpu.SMEM(source.shape, jnp.int32),
            pltpu.VMEM((len(chunks[0]) * TB, rows, width), BF),
            pltpu.VMEM((len(far) * TB * CAP, TB * rows), BF),
            table,
            dma((len(chunks[0]),)),
            dma(()),
        ],
        compiler_params=params,
        name="early",
    )(pltpu.with_memory_space_constraint(source, pltpu.HBM), tails)
    got = {}

    def launch(i, token=None):
        arrays = list(msgs[i])
        if token is not None:
            arrays, token = lax.optimization_barrier((arrays, token))
        got[i] = [send(a, engines, *rels[rel]) for a, rel in zip(arrays, far)]
        return token

    launch(0)
    lead = pl.pallas_call(
        functools.partial(lead_body, engines, rows),
        in_specs=[SM, ANY, ANY, VM, VM, VM, ANY],
        out_specs=[VM] * (1 + others),
        out_shape=[sds((4, rows, width), F32)] + [sds((CAP * (4 + modes), width), BF)] * others,
        scratch_shapes=[
            pltpu.VMEM((taps + 8, width), F32),
            pltpu.VMEM((tail_len, rows, width), BF),
            pltpu.VMEM((rows, modes, width), F32),
            table,
            dma((pl.cdiv(tail_len, TB),)),
            dma(()),
        ],
        compiler_params=params,
        name="lead",
    )(source, tails, modal_states, mr_filter, li_decay, li_residue, msgs[0][0])
    small = lead[1 : 1 + others]
    parts_got = [send(small[rel - 1], engines, *rels[rel]) for rel in range(1, engines)]

    sends = []
    for i in range(1, len(chunks)):
        sends += [(rel, chunks[i]) for rel in far]
    packed = pl.pallas_call(
        functools.partial(pack_body, engines, rows, sends),
        in_specs=[SM, ANY, VM],
        out_specs=[VM] * (3 + len(sends)),
        out_shape=[sds((blocks * TB * CAP, width), BF)]
        + [sds((len(group) * TB * CAP, width), BF) for _, group in sends]
        + [sds((TB * rows, TB * rows + others * TB * CAP), BF), sds((4, rows, width), F32)],
        scratch_shapes=[
            pltpu.VMEM((tail_len, rows, width), BF),
            pltpu.VMEM((others * TB * CAP, TB * rows), BF),
            table,
            table,
            tally,
            dma((blocks,)),
        ],
        compiler_params=params,
        name="pack",
    )(source, tails, lead[0])
    near_msg = packed[0]
    spread, parts = packed[-2:]
    msgs[1] = packed[1 : 1 + len(far)]
    msgs[2] = packed[1 + len(far) : 1 + 2 * len(far)]

    y, gates = pl.pallas_call(
        functools.partial(mix_body, engines, rows),
        in_specs=[SM] + [VM] * (6 + others) + [ANY] * (1 + len(far)),
        out_specs=[VM, VM],
        out_shape=[sds((4 * rows, width), BF), sds((4, rows, width), BF)],
        scratch_shapes=[pltpu.VMEM((4, rows, width), F32), table, tally],
        compiler_params=params,
        name="mix",
    )(source, parts, mr_qkv, li_qkv, mr_filter, li_decay, li_residue, *parts_got, spread, *got[0])

    near_msg, y = lax.optimization_barrier((near_msg, y))
    near_got = send(near_msg, engines, 0, 1)
    same_core = [y] + [send(y, engines, k, 0) for k in range(1, chips)]
    ys = []
    for k in range(chips):
        ys += [same_core[k], send(same_core[k], engines, 0, 1)]
    ys[1] = launch(1, ys[1])

    def place(i, arrays, layout, tails_so_far, kept=False):
        group = chunks[i]
        buffer = pltpu.VMEM((len(group), TB, rows, width), BF)
        carry = [] if kept else [gates if tails_so_far is None else tails_so_far]
        return pl.pallas_call(
            functools.partial(place_body, engines, rows, group, kept, layout),
            in_specs=[VM, VM, ANY] + [VM] * (1 + len(arrays)) + [ANY] * len(carry),
            out_specs=VM if kept else ANY,
            out_shape=sds(buffer.shape if kept else (tail_len, rows, width), BF),
            input_output_aliases={} if tails_so_far is None else {4 + len(arrays): 0},
            scratch_shapes=[buffer, dma((len(group),))]
            if kept
            else [buffer, pltpu.VMEM((len(group), TB + 2, rows, width), BF), dma((len(group),)), dma((len(group),))],
            compiler_params=params,
            name="place",
            cost_estimate=TINY,
        )(spread, gates, tails, near_got, *arrays, *carry)

    new_tails = place(0, got[0], [chunks[0]] * len(far), None)
    depth = 512
    outs = pl.pallas_call(
        functools.partial(project_body, engines, rows, slots_here, depth),
        grid=(width // depth,),
        in_specs=[pl.BlockSpec((4 * rows, width), lambda i: (0, 0))] * engines
        + [pl.BlockSpec((slots_here, depth, pw), lambda i: (0, i, 0))] * 2
        + [ANY],
        out_specs=[pl.BlockSpec((2 * rows, slots_here * pw), lambda i: (0, 0))] * engines,
        out_shape=[sds((2 * rows, slots_here * pw), BF)] * engines,
        scratch_shapes=[
            pltpu.VMEM((width // depth, 2, engines * 2 * rows, depth), BF),
            pltpu.VMEM((engines * 2 * rows, slots_here * pw), F32),
        ],
        compiler_params=params,
        name="project",
    )(*ys, mr_panels, li_panels, new_tails)

    back = [outs[0]]
    for k, f in rels[1:]:
        back.append(send(outs[2 * ((chips - k) % chips) + f], engines, k, f))
    got[1] = launch(2, got[1])

    new_states = pl.pallas_call(
        functools.partial(modal_body, engines, rows),
        in_specs=[SM, ANY, VM, VM] + [VM] * others,
        out_specs=ANY,
        out_shape=sds((rows, modes, width), F32),
        scratch_shapes=[
            pltpu.VMEM((rows, modes, width), F32),
            pltpu.VMEM((2, rows, width), F32),
            table,
            tally,
            dma((rows,)),
            dma((rows,)),
        ],
        compiler_params=params,
        name="modal",
        cost_estimate=TINY,
    )(source, modal_states, gates, li_decay, *parts_got)

    back[1], new_states = lax.optimization_barrier((back[1], new_states))
    per_chan = panel_slot.shape[0] // chans
    blocks_out = pl.pallas_call(
        functools.partial(sort_body, engines, chans, slots_here),
        in_specs=[SM] + [VM] * engines + [ANY] * len(far),
        out_specs=[VM] * chans,
        out_shape=[sds((2 * rows, per_chan * pw), BF)] * chans,
        scratch_shapes=[pltpu.VMEM((engines * slots_here, 2 * rows, pw), BF)],
        compiler_params=params,
        name="sort",
        cost_estimate=TINY,
    )(panel_slot, *back, *got[1])
    total = blocks_out[0].astype(F32)
    for d in range(1, chans):
        total = total + lax.ppermute(blocks_out[d], "chan", [(c, (c + d) % chans) for c in range(chans)]).astype(F32)
    steps_ids = jnp.arange(2, dtype=jnp.int32)
    active = (remaining[None, :] > steps_ids[:, None]).astype(F32)
    total, got[2][0] = lax.optimization_barrier((total, got[2][0]))
    mixed = (total.reshape(2, rows, per_chan * pw) * active[:, :, None]).astype(BF)

    new_tails = place(1, got[1], [chunks[1]] * len(far), new_tails)
    base = place(2, got[2][:-1], [chunks[2]] * (len(far) - 1), None, True)
    buffer = pltpu.VMEM((len(chunks[2]), TB, rows, width), BF)
    new_tails = pl.pallas_call(
        functools.partial(last_body, engines, rows, chunks[2]),
        in_specs=[VM, VM, VM, ANY],
        out_specs=ANY,
        out_shape=sds((tail_len, rows, width), BF),
        input_output_aliases={3: 0},
        scratch_shapes=[buffer, dma((len(chunks[2]),))],
        compiler_params=params,
        name="last",
        cost_estimate=TINY,
    )(spread, base, got[2][-1], new_tails)
    return (mixed, jnp.transpose(new_tails, (1, 0, 2)), new_states)


def solution(mesh):
    return jax.shard_map(
        body,
        mesh=mesh,
        in_specs=(
            P(None, None, ("group", "engine"), "chan"),
            P(None, None, ("group", "engine"), "chan"),
            P(("group", "engine"), None, "chan"),
            P(("group", "engine"), None, "chan"),
            P("group"),
            P(("group", "engine")),
            P(None, "chan"),
            P(None, "chan"),
            P(None, "chan"),
            P("engine", "chan", None),
            P("engine", "chan", None),
            P(),
        ),
        out_specs=(
            P(None, ("group", "engine"), "chan"),
            P(("group", "engine"), None, "chan"),
            P(("group", "engine"), None, "chan"),
        ),
        check_vma=False,
    )
```

```python
import functools

import jax
import jax.numpy as jnp
from jax import lax
from jax.experimental import pallas as pl
from jax.experimental.pallas import tpu as pltpu
from jax.sharding import PartitionSpec as P

CAP = 2
BF = jnp.bfloat16
F32 = jnp.float32
ANY = pl.BlockSpec(memory_space=pl.ANY)
SM = pl.BlockSpec(memory_space=pltpu.SMEM)
VM = pl.BlockSpec(memory_space=pltpu.VMEM)
VLIM = 48 << 20
TB = 16
TINY = pl.CostEstimate(flops=1, transcendentals=0, bytes_accessed=1)


def lane_chunk(width):
    for size in (256, 128):
        if width % size == 0:
            return size
    return width


def wide_chunk(width):
    return 1024 if width % 1024 == 0 else lane_chunk(width)


def links(engines):
    chips = engines // 2
    return [(k, f) for k in range(chips) for f in (0, 1)]


def send(x, engines, k, f):
    chips = engines // 2
    pairs = [(e, ((e // 2 + k) % chips) * 2 + ((e % 2) ^ f)) for e in range(engines)]
    return lax.ppermute(x, "engine", pairs)


def to_engine(me, k, f, engines):
    chips = engines // 2
    return lax.rem(lax.div(me, 2) + k, chips) * 2 + lax.rem(me + f, 2)


def relation_of(me, owner, engines):
    chips = engines // 2
    k = lax.rem(lax.div(me, 2) + chips - lax.div(owner, 2), chips)
    return 2 * k + lax.rem(owner + me, 2)


def departures(engines, rows, source, leave, me):
    for rel, (k, f) in enumerate(links(engines)):
        if rel == 0:
            continue
        there = to_engine(me, k, f, engines)
        for j in range(CAP):
            leave[rel * (CAP + 1) + j] = 0

        found = 0
        for i in range(rows):
            old = source[there * rows + i]
            leave[rel * (CAP + 1) + jnp.minimum(found, CAP)] = lax.rem(old, rows)
            found = found + jnp.where(lax.div(old, rows) == me, 1, 0)


def send_selector(rels, rows, leave, pick):
    height, depth = pick.shape
    at = lax.broadcasted_iota(jnp.int32, (height, 1), 0)
    group = at // (TB * CAP)
    tap = (at % (TB * CAP)) // CAP
    place = at % CAP
    row = jnp.zeros((height, 1), jnp.int32)
    for i, rel in enumerate(rels):
        for j in range(CAP):
            row = jnp.where((group == i) & (place == j), leave[rel * (CAP + 1) + j], row)
    want = tap * rows + row
    pick[...] = (lax.broadcasted_iota(jnp.int32, (height, depth), 1) == want).astype(F32).astype(BF)


def sent_taps(b, tail_len):
    return min(TB, tail_len - 3 - b * TB)


def early_body(engines, rows, blocks, source_far, tails, *refs):
    far = list(range(2, engines))
    msgs = refs[: len(far)]
    source, tbuf, pick, leave, tsem, source_sem = refs[len(far) :]
    tail_len, _, width = tails.shape
    chunk = wide_chunk(width)
    me = lax.axis_index("engine")

    def fetch(n):
        return pltpu.make_async_copy(tails.at[pl.ds(blocks[n] * TB, TB)], tbuf.at[pl.ds(n * TB, TB)], tsem.at[n])

    read = pltpu.make_async_copy(source_far, source, source_sem)
    read.start()
    for n in range(len(blocks)):
        fetch(n).start()
    read.wait()
    departures(engines, rows, source, leave, me)
    send_selector(far, rows, leave, pick)
    for n in range(len(blocks)):
        fetch(n).wait()

        for c in range(0, width, chunk):
            cols = pl.ds(c, chunk)
            old = tbuf[n * TB : (n + 1) * TB, :, cols].reshape(TB * rows, chunk)
            rowsel = jnp.dot(pick[...], old, preferred_element_type=F32).astype(BF)
            for i in range(len(far)):
                msgs[i][n * TB * CAP : (n + 1) * TB * CAP, cols] = rowsel[i * TB * CAP : (i + 1) * TB * CAP]


def lead_body(engines, rows, source, tails, states, filt, decay, resid, _, *refs):
    others = engines - 1
    parts = refs[0]
    small = refs[1 : 1 + others]
    fbuf, tbuf, sbuf, leave, tsem, ssem = refs[1 + others :]
    tail_len, _, width = tails.shape
    modes = states.shape[1]
    taps = filt.shape[0]
    chunk = wide_chunk(width)
    me = lax.axis_index("engine")
    total = pl.cdiv(tail_len, TB)

    def fetch(b):
        size = min(TB, tail_len - b * TB)
        return pltpu.make_async_copy(
            tails.at[pl.ds(b * TB, size)], tbuf.at[pl.ds(b * TB, size)], tsem.at[b]
        )

    for b in range(total):
        fetch(b).start()
    load_states = pltpu.make_async_copy(states, sbuf, ssem)
    load_states.start()
    departures(engines, rows, source, leave, me)
    for c in range(0, width, chunk):
        fbuf[0:taps, pl.ds(c, chunk)] = filt[:, pl.ds(c, chunk)].astype(F32)
        fbuf[taps : taps + 8, pl.ds(c, chunk)] = jnp.zeros((8, chunk), F32)
    for b in range(total):
        fetch(b).wait()
        size = min(TB, tail_len - b * TB)

        for c in range(0, width, chunk):
            cols = pl.ds(c, chunk)
            if b == 0:
                first = jnp.zeros((rows, chunk), F32)
                second = jnp.zeros((rows, chunk), F32)
            else:
                first = parts[0, :, cols]
                second = parts[1, :, cols]
            for i in range(size):
                t = tbuf[b * TB + i, :, cols].astype(F32)
                first += t * fbuf[b * TB + i + 1 : b * TB + i + 2, cols]
                second += t * fbuf[b * TB + i + 2 : b * TB + i + 3, cols]
            parts[0, :, cols] = first
            parts[1, :, cols] = second
    parts[4] = tbuf[tail_len - 3].astype(F32)
    load_states.wait()

    def modal(r, carry):
        s = sbuf[r]
        a = resid[...] * (decay[...] * s)
        parts[2, pl.ds(r, 1), :] = jnp.sum(a, axis=0, keepdims=True)
        parts[3, pl.ds(r, 1), :] = jnp.sum(a * decay[...], axis=0, keepdims=True)
        return carry

    lax.fori_loop(0, rows, modal, 0)
    for rel in range(1, engines):
        for j in range(CAP):
            old = leave[rel * (CAP + 1) + j]
            small[rel - 1][j * modes : (j + 1) * modes, :] = sbuf[old].astype(BF)
            for n, i in enumerate((0, 1, 4)):
                at = CAP * modes + 3 * j + n
                small[rel - 1][at : at + 1, :] = parts[i, pl.ds(old, 1), :].astype(BF)


def pack_body(engines, rows, sends, source, tails, parts_in, *refs):
    far = list(range(2, engines))
    near = refs[0]
    msgs = refs[1 : 1 + len(sends)]
    spread, parts, tbuf, pick, leave, slots, found, tsem = refs[1 + len(msgs) :]
    tail_len, _, width = tails.shape
    chunk = wide_chunk(width)
    me = lax.axis_index("engine")
    total = pl.cdiv(tail_len - 3, TB)
    others = engines - 1

    def fetch(b):
        n = sent_taps(b, tail_len)
        return pltpu.make_async_copy(tails.at[pl.ds(b * TB, n)], tbuf.at[pl.ds(b * TB, n)], tsem.at[b])

    for b in range(total):
        fetch(b).start()
    departures(engines, rows, source, leave, me)
    send_selector([1] + far, rows, leave, pick)
    arrivals(engines, rows, source, slots, found, me)
    height, depth = spread.shape
    at = lax.broadcasted_iota(jnp.int32, (height, 1), 0)
    tap = at // rows
    new_row = at % rows
    want = jnp.zeros((height, 1), jnp.int32)
    for r in range(rows):
        old = source[me * rows + r]
        want = jnp.where(new_row == r, tap * rows + old % rows, want)
    for rel in range(1, engines):
        for j in range(CAP):
            row = jnp.where(found[rel] > j, slots[rel * (CAP + 1) + j], -1)
            want = jnp.where(new_row == row, TB * rows + (rel - 1) * TB * CAP + CAP * tap + j, want)
    spread[...] = (lax.broadcasted_iota(jnp.int32, (height, depth), 1) == want).astype(F32).astype(BF)

    def stay(r, carry):
        old = lax.rem(source[me * rows + r], rows)
        for i in range(5):
            parts[i, pl.ds(r, 1), :] = parts_in[i, pl.ds(old, 1), :]
        return carry

    lax.fori_loop(0, rows, stay, 0)
    for b in range(total):
        fetch(b).wait()
        n = sent_taps(b, tail_len)
        home = [(msg, rel, blocks) for msg, (rel, blocks) in zip(msgs, sends) if b in blocks]
        tall = pick.shape[0] if home else TB * CAP
        for c in range(0, width, chunk):
            cols = pl.ds(c, chunk)
            old = tbuf[b * TB : b * TB + n, :, cols].reshape(n * rows, chunk)
            rowsel = jnp.dot(pick[0:tall, 0 : n * rows], old, preferred_element_type=F32).astype(BF)
            near[b * TB * CAP : (b + 1) * TB * CAP, cols] = rowsel[0 : TB * CAP]
            for msg, rel, blocks in home:
                base = (b - blocks[0]) * TB * CAP
                msg[base : base + n * CAP, cols] = rowsel[(rel - 1) * TB * CAP : (rel - 1) * TB * CAP + n * CAP]


def arrivals(engines, rows, source, slots, found, me):
    for rel in range(engines):
        found[rel] = 0
    for r in range(rows):
        rel = relation_of(me, lax.div(source[me * rows + r], rows), engines)
        at = found[rel]
        slots[rel * (CAP + 1) + jnp.minimum(at, CAP)] = r
        found[rel] = at + 1


def mix_body(engines, rows, source, parts_in, mr, li, filt, decay, resid, *refs):
    got = refs[: engines - 1]
    y, gates, parts, slots, found = refs[-5:]
    width = y.shape[1]
    modes = decay.shape[0]
    chunk = lane_chunk(width)
    me = lax.axis_index("engine")
    arrivals(engines, rows, source, slots, found, me)

    parts[...] = parts_in[...]
    for rel in range(1, engines):
        for j in range(CAP):

            @pl.when(found[rel] > j)
            def _():
                one = pl.ds(slots[rel * (CAP + 1) + j], 1)
                for n, i in enumerate((0, 1, 4)):
                    at = CAP * modes + 3 * j + n
                    parts[i, one, :] = got[rel - 1][at : at + 1, :].astype(F32)
                for c in range(0, width, chunk):
                    cols = pl.ds(c, chunk)
                    d = decay[:, cols]
                    a = resid[:, cols] * (d * got[rel - 1][j * modes : (j + 1) * modes, cols].astype(F32))
                    parts[2, one, cols] = jnp.sum(a, axis=0, keepdims=True)
                    parts[3, one, cols] = jnp.sum(a * d, axis=0, keepdims=True)

    gates[4] = parts[4].astype(BF)
    for c in range(0, width, chunk):
        cols = pl.ds(c, chunk)
        f = filt[0:16, cols].astype(F32)
        d = decay[:, cols]
        w = resid[:, cols]
        r0 = jnp.sum(w, axis=0, keepdims=True)
        r1 = jnp.sum(w * d, axis=0, keepdims=True)
        z = []
        for n, qkv in enumerate((mr, mr, li, li)):
            gate = (qkv[n % 2, 1, :, cols].astype(F32) * qkv[n % 2, 2, :, cols].astype(F32)).astype(BF)
            gates[n, :, cols] = gate
            z.append(gate.astype(F32))
        conv0 = f[0:1] * z[0] + parts[0, :, cols]
        conv1 = f[0:1] * z[1] + f[1:2] * z[0] + parts[1, :, cols]
        y[0:rows, cols] = (mr[0, 0, :, cols].astype(F32) * conv0).astype(BF)
        y[rows : 2 * rows, cols] = (mr[1, 0, :, cols].astype(F32) * conv1).astype(BF)
        modal0 = parts[2, :, cols] + z[2] * r0
        modal1 = parts[3, :, cols] + z[2] * r1 + z[3] * r0
        y[2 * rows : 3 * rows, cols] = (li[0, 0, :, cols].astype(F32) * modal0).astype(BF)
        y[3 * rows : 4 * rows, cols] = (li[1, 0, :, cols].astype(F32) * modal1).astype(BF)


def project_body(engines, rows, slots_here, depth, *refs):
    ys = refs[:engines]
    mr_w, li_w = refs[engines : engines + 2]
    outs = refs[-2 - engines : -2]
    x, acc = refs[-2:]
    two = 2 * rows
    width = ys[0].shape[1]
    pw = mr_w.shape[2]
    step = pl.program_id(0)

    @pl.when(step == 0)
    def _():
        for rel in range(engines):
            for b in range(width // depth):
                x[b, 0, rel * two : (rel + 1) * two, :] = ys[rel][0:two, b * depth : (b + 1) * depth]
                x[b, 1, rel * two : (rel + 1) * two, :] = ys[rel][two : 2 * two, b * depth : (b + 1) * depth]
        acc[...] = jnp.zeros_like(acc)

    for g in range(slots_here):
        cols = slice(g * pw, (g + 1) * pw)
        acc[:, cols] += jnp.dot(x[step, 0], mr_w[g], preferred_element_type=F32) + jnp.dot(
            x[step, 1], li_w[g], preferred_element_type=F32
        )

    @pl.when(step == pl.num_programs(0) - 1)
    def _():
        for rel in range(engines):
            outs[rel][...] = acc[rel * two : (rel + 1) * two, :].astype(BF)


def sort_body(engines, chans, slots_here, slot_of, *refs):
    got = refs[:engines]
    outs = refs[-1 - chans : -1]
    tiles = refs[-1]
    pw = tiles.shape[2]
    me = lax.axis_index("engine")
    here = lax.axis_index("chan")
    per_chan = slot_of.shape[0] // chans
    for rel in range(engines):
        for g in range(slots_here):
            tiles[rel * slots_here + g] = got[rel][:, g * pw : (g + 1) * pw]
    for d in range(chans):
        there = (here + d) % chans
        for h in range(per_chan):
            slot = slot_of[there * per_chan + h]
            rel = relation_of(me, slot // slots_here, engines)
            outs[d][:, h * pw : (h + 1) * pw] = tiles[rel * slots_here + slot % slots_here]


def place_body(engines, rows, blocks, kept, layout, spread, gates, tails, near, *refs):
    msgs = refs[: len(layout)]
    if kept:
        new, tbuf, isem = refs[len(layout) :]
    else:
        new, tbuf, obuf, isem, osem = refs[len(layout) + 1 :]
    tail_len, _, width = tails.shape
    chunk = wide_chunk(width)
    lead = 2 if blocks[0] == 0 else 0

    def fetch(n):
        b = blocks[n]
        taps = sent_taps(b, tail_len)
        return pltpu.make_async_copy(tails.at[pl.ds(b * TB, taps)], tbuf.at[n, pl.ds(0, taps)], isem.at[n])

    def store(n):
        b = blocks[n]
        taps = sent_taps(b, tail_len)
        extra = lead if n == 0 else 0
        return pltpu.make_async_copy(
            obuf.at[n, pl.ds(2 - extra, taps + extra)], new.at[pl.ds(b * TB + 2 - extra, taps + extra)], osem.at[n]
        )

    for n in range(len(blocks)):
        fetch(n).start()
    if lead:
        obuf[0, 0] = gates[1]
        obuf[0, 1] = gates[0]
        edge = pltpu.make_async_copy(gates.at[4], new.at[tail_len - 1], osem.at[len(blocks)])
        edge.start()
    for n, b in enumerate(blocks):
        fetch(n).wait()
        taps = sent_taps(b, tail_len)
        top = taps * rows
        for c in range(0, width, chunk):
            cols = pl.ds(c, chunk)
            old = tbuf[n, 0:taps, :, cols].reshape(top, chunk)
            pieces = [near[b * TB * CAP : b * TB * CAP + taps * CAP, cols]]
            for msg, held in zip(msgs, layout):
                if b in held:
                    base = (b - held[0]) * TB * CAP
                    pieces.append(msg[base : base + taps * CAP, cols])
            if taps == TB:
                pieces = [jnp.concatenate(pieces, axis=0)]
            value = jnp.dot(spread[0:top, 0:top], old, preferred_element_type=F32)
            for i, piece in enumerate(pieces):
                left = TB * rows + i * TB * CAP
                value += jnp.dot(
                    spread[0:top, left : left + piece.shape[0]], piece, preferred_element_type=F32
                )
            value = value.astype(BF).reshape(taps, rows, chunk)
            if kept:
                new[n, 0:taps, :, cols] = value
            else:
                obuf[n, 2 : 2 + taps, :, cols] = value
        if not kept:
            store(n).start()
    if not kept:
        for n in range(len(blocks)):
            store(n).wait()
    if lead:
        edge.wait()


def last_body(engines, rows, blocks, spread, base, msg, _, new_tails, obuf, osem):
    tail_len, _, width = new_tails.shape
    chunk = wide_chunk(width)

    def store(n):
        b = blocks[n]
        taps = sent_taps(b, tail_len)
        return pltpu.make_async_copy(obuf.at[n, pl.ds(0, taps)], new_tails.at[pl.ds(b * TB + 2, taps)], osem.at[n])

    left = spread.shape[1] - TB * CAP
    for n, b in enumerate(blocks):
        taps = sent_taps(b, tail_len)
        top = taps * rows
        for c in range(0, width, chunk):
            cols = pl.ds(c, chunk)
            value = jnp.dot(
                spread[0:top, left : left + taps * CAP],
                msg[n * TB * CAP : n * TB * CAP + taps * CAP, cols],
                preferred_element_type=F32,
            )
            value = value + base[n, 0:taps, :, cols].reshape(top, chunk).astype(F32)
            obuf[n, 0:taps, :, cols] = value.astype(BF).reshape(taps, rows, chunk)
        store(n).start()
    for n in range(len(blocks)):
        store(n).wait()


def modal_body(engines, rows, source, states, gates, decay, *refs):
    others = engines - 1
    msgs = refs[:others]
    new_states = refs[others]
    sbuf, z, slots, found, isem, osem = refs[others + 1 :]
    modes = states.shape[1]
    me = lax.axis_index("engine")

    def fetch(r):
        return pltpu.make_async_copy(states.at[lax.rem(source[me * rows + r], rows)], sbuf.at[r], isem.at[r])

    def store(r):
        return pltpu.make_async_copy(sbuf.at[r], new_states.at[r], osem.at[r])

    def stays(r):
        return lax.div(source[me * rows + r], rows) == me

    def begin(r, carry):
        @pl.when(stays(r))
        def _():
            fetch(r).start()

        return carry

    lax.fori_loop(0, rows, begin, 0)
    z[...] = gates[2:4].astype(F32)
    arrivals(engines, rows, source, slots, found, me)

    def advance(r, s):
        d = decay[...]
        sbuf[r] = d * (d * s + z[0, pl.ds(r, 1), :]) + z[1, pl.ds(r, 1), :]
        store(r).start()

    for rel in range(1, engines):
        for j in range(CAP):

            @pl.when(found[rel] > j)
            def _():
                base = j * modes
                advance(slots[rel * (CAP + 1) + j], msgs[rel - 1][base : base + modes, :].astype(F32))

    def work(r, carry):
        @pl.when(stays(r))
        def _():
            fetch(r).wait()
            advance(r, sbuf[r])

        return carry

    lax.fori_loop(0, rows, work, 0)

    def finish(r, carry):
        store(r).wait()
        return carry

    lax.fori_loop(0, rows, finish, 0)


def split(total):
    cuts = [0, 2 * total // 8, 5 * total // 8, total]
    return [list(range(a, b)) for a, b in zip(cuts, cuts[1:]) if a < b]


def body(mr_qkv, li_qkv, conv_tails, modal_states, source, remaining, mr_filter, li_decay, li_residue, mr_panels,
         li_panels, panel_slot):
    engines = lax.axis_size("engine")
    chans = lax.axis_size("chan")
    rows, tail_len, width = conv_tails.shape
    modes = modal_states.shape[1]
    taps = mr_filter.shape[0]
    slots_here, _, pw = mr_panels.shape
    others = engines - 1
    chips = engines // 2
    rels = links(engines)
    far = list(range(2, engines))
    sds = jax.ShapeDtypeStruct
    dma = pltpu.SemaphoreType.DMA
    params = pltpu.CompilerParams(vmem_limit_bytes=VLIM)
    tails = jnp.transpose(conv_tails, (1, 0, 2))
    blocks = pl.cdiv(tail_len - 3, TB)
    chunks = split(blocks)
    table = pltpu.SMEM((engines * (CAP + 1),), jnp.int32)
    tally = pltpu.SMEM((engines,), jnp.int32)

    def msg_rows(i):
        return len(chunks[i]) * TB * CAP

    msgs = {}
    msgs[0] = pl.pallas_call(
        functools.partial(early_body, engines, rows, chunks[0]),
        in_specs=[ANY, ANY],
        out_specs=[VM] * len(far),
        out_shape=[sds((msg_rows(0), width), BF)] * len(far),
        scratch_shapes=[
            pltpu.SMEM(source.shape, jnp.int32),
            pltpu.VMEM((len(chunks[0]) * TB, rows, width), BF),
            pltpu.VMEM((len(far) * TB * CAP, TB * rows), BF),
            table,
            dma((len(chunks[0]),)),
            dma(()),
        ],
        compiler_params=params,
        name="early",
    )(pltpu.with_memory_space_constraint(source, pltpu.HBM), tails)
    got = {}

    def launch(i, token=None):
        arrays = list(msgs[i])
        if token is not None:
            arrays, token = lax.optimization_barrier((arrays, token))
        got[i] = [send(a, engines, *rels[rel]) for a, rel in zip(arrays, far)]
        return token

    launch(0)
    lead = pl.pallas_call(
        functools.partial(lead_body, engines, rows),
        in_specs=[SM, ANY, ANY, VM, VM, VM, ANY],
        out_specs=[VM] * (1 + others),
        out_shape=[sds((5, rows, width), F32)] + [sds((pl.cdiv(CAP * (3 + modes), 8) * 8, width), BF)] * others,
        scratch_shapes=[
            pltpu.VMEM((taps + 8, width), F32),
            pltpu.VMEM((tail_len, rows, width), BF),
            pltpu.VMEM((rows, modes, width), F32),
            table,
            dma((pl.cdiv(tail_len, TB),)),
            dma(()),
        ],
        compiler_params=params,
        name="lead",
    )(source, tails, modal_states, mr_filter, li_decay, li_residue, msgs[0][0])
    small = lead[1 : 1 + others]
    parts_got = [send(small[rel - 1], engines, *rels[rel]) for rel in range(1, engines)]

    sends = []
    for i in range(1, len(chunks)):
        sends += [(rel, chunks[i]) for rel in far]
    packed = pl.pallas_call(
        functools.partial(pack_body, engines, rows, sends),
        in_specs=[SM, ANY, VM],
        out_specs=[VM] * (3 + len(sends)),
        out_shape=[sds((blocks * TB * CAP, width), BF)]
        + [sds((CAP * sum(sent_taps(b, tail_len) for b in group), width), BF) for _, group in sends]
        + [sds((TB * rows, TB * rows + others * TB * CAP), BF), sds((5, rows, width), F32)],
        scratch_shapes=[
            pltpu.VMEM((tail_len, rows, width), BF),
            pltpu.VMEM((others * TB * CAP, TB * rows), BF),
            table,
            table,
            tally,
            dma((blocks,)),
        ],
        compiler_params=params,
        name="pack",
    )(source, tails, lead[0])
    near_msg = packed[0]
    spread, parts = packed[-2:]
    msgs[1] = packed[1 : 1 + len(far)]
    msgs[2] = packed[1 + len(far) : 1 + 2 * len(far)]

    y, gates = pl.pallas_call(
        functools.partial(mix_body, engines, rows),
        in_specs=[SM] + [VM] * (6 + others) + [ANY] * (1 + len(far)),
        out_specs=[VM, VM],
        out_shape=[sds((4 * rows, width), BF), sds((5, rows, width), BF)],
        scratch_shapes=[pltpu.VMEM((5, rows, width), F32), table, tally],
        compiler_params=params,
        name="mix",
    )(source, parts, mr_qkv, li_qkv, mr_filter, li_decay, li_residue, *parts_got, spread, *got[0])

    near_msg, y = lax.optimization_barrier((near_msg, y))
    near_got = send(near_msg, engines, 0, 1)
    same_core = [y] + [send(y, engines, k, 0) for k in range(1, chips)]
    ys = []
    for k in range(chips):
        ys += [same_core[k], send(same_core[k], engines, 0, 1)]
    ys[1] = launch(1, ys[1])

    def place(i, arrays, layout, tails_so_far, kept=False):
        group = chunks[i]
        buffer = pltpu.VMEM((len(group), TB, rows, width), BF)
        carry = [] if kept else [gates if tails_so_far is None else tails_so_far]
        return pl.pallas_call(
            functools.partial(place_body, engines, rows, group, kept, layout),
            in_specs=[VM, VM, ANY] + [VM] * (1 + len(arrays)) + [ANY] * len(carry),
            out_specs=VM if kept else ANY,
            out_shape=sds(buffer.shape if kept else (tail_len, rows, width), BF),
            input_output_aliases={} if tails_so_far is None else {4 + len(arrays): 0},
            scratch_shapes=[buffer, dma((len(group),))]
            if kept
            else [buffer, pltpu.VMEM((len(group), TB + 2, rows, width), BF), dma((len(group),)), dma((len(group) + 1,))],
            compiler_params=params,
            name="place",
            cost_estimate=TINY,
        )(spread, gates, tails, near_got, *arrays, *carry)

    new_tails = place(0, got[0], [chunks[0]] * len(far), None)
    depth = 512
    outs = pl.pallas_call(
        functools.partial(project_body, engines, rows, slots_here, depth),
        grid=(width // depth,),
        in_specs=[pl.BlockSpec((4 * rows, width), lambda i: (0, 0))] * engines
        + [pl.BlockSpec((slots_here, depth, pw), lambda i: (0, i, 0))] * 2
        + [ANY],
        out_specs=[pl.BlockSpec((2 * rows, slots_here * pw), lambda i: (0, 0))] * engines,
        out_shape=[sds((2 * rows, slots_here * pw), BF)] * engines,
        scratch_shapes=[
            pltpu.VMEM((width // depth, 2, engines * 2 * rows, depth), BF),
            pltpu.VMEM((engines * 2 * rows, slots_here * pw), F32),
        ],
        compiler_params=params,
        name="project",
    )(*ys, mr_panels, li_panels, new_tails)

    back = [outs[0]]
    for k, f in rels[1:]:
        back.append(send(outs[2 * ((chips - k) % chips) + f], engines, k, f))
    got[1] = launch(2, got[1])

    new_states = pl.pallas_call(
        functools.partial(modal_body, engines, rows),
        in_specs=[SM, ANY, VM, VM] + [VM] * others,
        out_specs=ANY,
        out_shape=sds((rows, modes, width), F32),
        scratch_shapes=[
            pltpu.VMEM((rows, modes, width), F32),
            pltpu.VMEM((2, rows, width), F32),
            table,
            tally,
            dma((rows,)),
            dma((rows,)),
        ],
        compiler_params=params,
        name="modal",
        cost_estimate=TINY,
    )(source, modal_states, gates, li_decay, *parts_got)

    back[1], new_states = lax.optimization_barrier((back[1], new_states))
    per_chan = panel_slot.shape[0] // chans
    blocks_out = pl.pallas_call(
        functools.partial(sort_body, engines, chans, slots_here),
        in_specs=[SM] + [VM] * engines + [ANY] * len(far),
        out_specs=[VM] * chans,
        out_shape=[sds((2 * rows, per_chan * pw), BF)] * chans,
        scratch_shapes=[pltpu.VMEM((engines * slots_here, 2 * rows, pw), BF)],
        compiler_params=params,
        name="sort",
        cost_estimate=TINY,
    )(panel_slot, *back, *got[1])
    total = blocks_out[0].astype(F32)
    for d in range(1, chans):
        total = total + lax.ppermute(blocks_out[d], "chan", [(c, (c + d) % chans) for c in range(chans)]).astype(F32)
    steps_ids = jnp.arange(2, dtype=jnp.int32)
    active = (remaining[None, :] > steps_ids[:, None]).astype(F32)
    total, got[2][0] = lax.optimization_barrier((total, got[2][0]))
    mixed = (total.reshape(2, rows, per_chan * pw) * active[:, :, None]).astype(BF)

    new_tails = place(1, got[1], [chunks[1]] * len(far), new_tails)
    base = place(2, got[2][:-1], [chunks[2]] * (len(far) - 1), None, True)
    buffer = pltpu.VMEM((len(chunks[2]), TB, rows, width), BF)
    new_tails = pl.pallas_call(
        functools.partial(last_body, engines, rows, chunks[2]),
        in_specs=[VM, VM, VM, ANY],
        out_specs=ANY,
        out_shape=sds((tail_len, rows, width), BF),
        input_output_aliases={3: 0},
        scratch_shapes=[buffer, dma((len(chunks[2]),))],
        compiler_params=params,
        name="last",
        cost_estimate=TINY,
    )(spread, base, got[2][-1], new_tails)
    return (mixed, jnp.transpose(new_tails, (1, 0, 2)), new_states)


def solution(mesh):
    return jax.shard_map(
        body,
        mesh=mesh,
        in_specs=(
            P(None, None, ("group", "engine"), "chan"),
            P(None, None, ("group", "engine"), "chan"),
            P(("group", "engine"), None, "chan"),
            P(("group", "engine"), None, "chan"),
            P("group"),
            P(("group", "engine")),
            P(None, "chan"),
            P(None, "chan"),
            P(None, "chan"),
            P("engine", "chan", None),
            P("engine", "chan", None),
            P(),
        ),
        out_specs=(
            P(None, ("group", "engine"), "chan"),
            P(("group", "engine"), None, "chan"),
            P(("group", "engine"), None, "chan"),
        ),
        check_vma=False,
    )
```

```python
import functools

import jax
import jax.numpy as jnp
from jax import lax
from jax.experimental import pallas as pl
from jax.experimental.pallas import tpu as pltpu
from jax.sharding import PartitionSpec as P

CAP = 2
BF = jnp.bfloat16
F32 = jnp.float32
ANY = pl.BlockSpec(memory_space=pl.ANY)
SM = pl.BlockSpec(memory_space=pltpu.SMEM)
VM = pl.BlockSpec(memory_space=pltpu.VMEM)
VLIM = 48 << 20
TB = 16
TINY = pl.CostEstimate(flops=1, transcendentals=0, bytes_accessed=1)


def lane_chunk(width):
    for size in (256, 128):
        if width % size == 0:
            return size
    return width


def wide_chunk(width):
    return 1024 if width % 1024 == 0 else lane_chunk(width)


def links(engines):
    chips = engines // 2
    return [(k, f) for k in range(chips) for f in (0, 1)]


def send(x, engines, k, f):
    chips = engines // 2
    pairs = [(e, ((e // 2 + k) % chips) * 2 + ((e % 2) ^ f)) for e in range(engines)]
    return lax.ppermute(x, "engine", pairs)


def to_engine(me, k, f, engines):
    chips = engines // 2
    return lax.rem(lax.div(me, 2) + k, chips) * 2 + lax.rem(me + f, 2)


def relation_of(me, owner, engines):
    chips = engines // 2
    k = lax.rem(lax.div(me, 2) + chips - lax.div(owner, 2), chips)
    return 2 * k + lax.rem(owner + me, 2)


def departures(engines, rows, source, leave, me):
    for rel, (k, f) in enumerate(links(engines)):
        if rel == 0:
            continue
        there = to_engine(me, k, f, engines)
        for j in range(CAP):
            leave[rel * (CAP + 1) + j] = 0

        found = 0
        for i in range(rows):
            old = source[there * rows + i]
            leave[rel * (CAP + 1) + jnp.minimum(found, CAP)] = lax.rem(old, rows)
            found = found + jnp.where(lax.div(old, rows) == me, 1, 0)


def send_selector(rels, rows, leave, pick):
    height, depth = pick.shape
    at = lax.broadcasted_iota(jnp.int32, (height, 1), 0)
    group = at // (TB * CAP)
    tap = (at % (TB * CAP)) // CAP
    place = at % CAP
    row = jnp.zeros((height, 1), jnp.int32)
    for i, rel in enumerate(rels):
        for j in range(CAP):
            row = jnp.where((group == i) & (place == j), leave[rel * (CAP + 1) + j], row)
    want = tap * rows + row
    pick[...] = (lax.broadcasted_iota(jnp.int32, (height, depth), 1) == want).astype(F32).astype(BF)


def sent_taps(b, tail_len):
    return min(TB, tail_len - 3 - b * TB)


def early_body(engines, rows, blocks, source_far, tails, *refs):
    far = list(range(2, engines))
    msgs = refs[: len(far)]
    source, tbuf, pick, leave, tsem, source_sem = refs[len(far) :]
    tail_len, _, width = tails.shape
    chunk = wide_chunk(width)
    me = lax.axis_index("engine")

    def fetch(n):
        return pltpu.make_async_copy(tails.at[pl.ds(blocks[n] * TB, TB)], tbuf.at[pl.ds(n * TB, TB)], tsem.at[n])

    read = pltpu.make_async_copy(source_far, source, source_sem)
    read.start()
    for n in range(len(blocks)):
        fetch(n).start()
    read.wait()
    departures(engines, rows, source, leave, me)
    send_selector(far, rows, leave, pick)
    for n in range(len(blocks)):
        fetch(n).wait()

        for c in range(0, width, chunk):
            cols = pl.ds(c, chunk)
            old = tbuf[n * TB : (n + 1) * TB, :, cols].reshape(TB * rows, chunk)
            rowsel = jnp.dot(pick[...], old, preferred_element_type=F32).astype(BF)
            for i in range(len(far)):
                msgs[i][n * TB * CAP : (n + 1) * TB * CAP, cols] = rowsel[i * TB * CAP : (i + 1) * TB * CAP]


def lead_body(engines, rows, source, tails, states, filt, decay, resid, _, *refs):
    others = engines - 1
    parts = refs[0]
    small = refs[1 : 1 + others]
    fbuf, tbuf, sbuf, leave, tsem, ssem = refs[1 + others :]
    tail_len, _, width = tails.shape
    modes = states.shape[1]
    taps = filt.shape[0]
    chunk = wide_chunk(width)
    me = lax.axis_index("engine")
    total = pl.cdiv(tail_len, TB)

    def fetch(b):
        size = min(TB, tail_len - b * TB)
        return pltpu.make_async_copy(
            tails.at[pl.ds(b * TB, size)], tbuf.at[pl.ds(b * TB, size)], tsem.at[b]
        )

    for b in range(total):
        fetch(b).start()
    load_states = pltpu.make_async_copy(states, sbuf, ssem)
    load_states.start()
    departures(engines, rows, source, leave, me)
    for c in range(0, width, chunk):
        fbuf[0:taps, pl.ds(c, chunk)] = filt[:, pl.ds(c, chunk)].astype(F32)
        fbuf[taps : taps + 8, pl.ds(c, chunk)] = jnp.zeros((8, chunk), F32)
    for b in range(total):
        fetch(b).wait()
        size = min(TB, tail_len - b * TB)

        for c in range(0, width, chunk):
            cols = pl.ds(c, chunk)
            if b == 0:
                first = jnp.zeros((rows, chunk), F32)
                second = jnp.zeros((rows, chunk), F32)
            else:
                first = parts[0, :, cols]
                second = parts[1, :, cols]
            for i in range(size):
                t = tbuf[b * TB + i, :, cols].astype(F32)
                first += t * fbuf[b * TB + i + 1 : b * TB + i + 2, cols]
                second += t * fbuf[b * TB + i + 2 : b * TB + i + 3, cols]
            parts[0, :, cols] = first
            parts[1, :, cols] = second
    parts[4] = tbuf[tail_len - 3].astype(F32)
    load_states.wait()

    def modal(r, carry):
        s = sbuf[r]
        a = resid[...] * (decay[...] * s)
        parts[2, pl.ds(r, 1), :] = jnp.sum(a, axis=0, keepdims=True)
        parts[3, pl.ds(r, 1), :] = jnp.sum(a * decay[...], axis=0, keepdims=True)
        return carry

    lax.fori_loop(0, rows, modal, 0)
    for rel in range(1, engines):
        for j in range(CAP):
            old = leave[rel * (CAP + 1) + j]
            small[rel - 1][j * modes : (j + 1) * modes, :] = sbuf[old].astype(BF)
            for n, i in enumerate((0, 1, 4)):
                at = CAP * modes + 3 * j + n
                small[rel - 1][at : at + 1, :] = parts[i, pl.ds(old, 1), :].astype(BF)


def pack_body(engines, rows, sends, source, tails, parts_in, *refs):
    far = list(range(2, engines))
    near = refs[0]
    msgs = refs[1 : 1 + len(sends)]
    spread, parts, slots, found, tbuf, pick, leave, tsem = refs[1 + len(msgs) :]
    tail_len, _, width = tails.shape
    chunk = wide_chunk(width)
    me = lax.axis_index("engine")
    total = pl.cdiv(tail_len - 3, TB)
    others = engines - 1

    def fetch(b):
        n = sent_taps(b, tail_len)
        return pltpu.make_async_copy(tails.at[pl.ds(b * TB, n)], tbuf.at[pl.ds(b * TB, n)], tsem.at[b])

    for b in range(total):
        fetch(b).start()
    departures(engines, rows, source, leave, me)
    send_selector([1] + far, rows, leave, pick)
    arrivals(engines, rows, source, slots, found, me)
    height, depth = spread.shape
    at = lax.broadcasted_iota(jnp.int32, (height, 1), 0)
    tap = at // rows
    new_row = at % rows
    want = jnp.zeros((height, 1), jnp.int32)
    for r in range(rows):
        old = source[me * rows + r]
        want = jnp.where(new_row == r, tap * rows + old % rows, want)
    for rel in range(1, engines):
        for j in range(CAP):
            row = jnp.where(found[rel] > j, slots[rel * (CAP + 1) + j], -1)
            want = jnp.where(new_row == row, TB * rows + (rel - 1) * TB * CAP + CAP * tap + j, want)
    spread[...] = (lax.broadcasted_iota(jnp.int32, (height, depth), 1) == want).astype(F32).astype(BF)

    def stay(r, carry):
        old = lax.rem(source[me * rows + r], rows)
        for i in range(5):
            parts[i, pl.ds(r, 1), :] = parts_in[i, pl.ds(old, 1), :]
        return carry

    lax.fori_loop(0, rows, stay, 0)
    for b in range(total):
        fetch(b).wait()
        n = sent_taps(b, tail_len)
        home = [(msg, rel, blocks) for msg, (rel, blocks) in zip(msgs, sends) if b in blocks]
        tall = pick.shape[0] if home else TB * CAP
        for c in range(0, width, chunk):
            cols = pl.ds(c, chunk)
            old = tbuf[b * TB : b * TB + n, :, cols].reshape(n * rows, chunk)
            rowsel = jnp.dot(pick[0:tall, 0 : n * rows], old, preferred_element_type=F32).astype(BF)
            near[b * TB * CAP : (b + 1) * TB * CAP, cols] = rowsel[0 : TB * CAP]
            for msg, rel, blocks in home:
                base = (b - blocks[0]) * TB * CAP
                msg[base : base + n * CAP, cols] = rowsel[(rel - 1) * TB * CAP : (rel - 1) * TB * CAP + n * CAP]


def arrivals(engines, rows, source, slots, found, me):
    for rel in range(engines):
        found[rel] = 0
    for r in range(rows):
        rel = relation_of(me, lax.div(source[me * rows + r], rows), engines)
        at = found[rel]
        slots[rel * (CAP + 1) + jnp.minimum(at, CAP)] = r
        found[rel] = at + 1


def mix_body(engines, rows, slots, found, parts_in, mr, li, filt, decay, resid, *refs):
    got = refs[: engines - 1]
    y, gates, parts = refs[-3:]
    width = y.shape[1]
    modes = decay.shape[0]
    chunk = lane_chunk(width)

    parts[...] = parts_in[...]
    for rel in range(1, engines):
        for j in range(CAP):

            @pl.when(found[rel] > j)
            def _():
                one = pl.ds(slots[rel * (CAP + 1) + j], 1)
                for n, i in enumerate((0, 1, 4)):
                    at = CAP * modes + 3 * j + n
                    parts[i, one, :] = got[rel - 1][at : at + 1, :].astype(F32)
                for c in range(0, width, wide_chunk(width)):
                    cols = pl.ds(c, wide_chunk(width))
                    d = decay[:, cols]
                    a = resid[:, cols] * (d * got[rel - 1][j * modes : (j + 1) * modes, cols].astype(F32))
                    parts[2, one, cols] = jnp.sum(a, axis=0, keepdims=True)
                    parts[3, one, cols] = jnp.sum(a * d, axis=0, keepdims=True)

    gates[4] = parts[4].astype(BF)
    for c in range(0, width, chunk):
        cols = pl.ds(c, chunk)
        f = filt[0:16, cols].astype(F32)
        d = decay[:, cols]
        w = resid[:, cols]
        r0 = jnp.sum(w, axis=0, keepdims=True)
        r1 = jnp.sum(w * d, axis=0, keepdims=True)
        z = []
        for n, qkv in enumerate((mr, mr, li, li)):
            gate = (qkv[n % 2, 1, :, cols].astype(F32) * qkv[n % 2, 2, :, cols].astype(F32)).astype(BF)
            gates[n, :, cols] = gate
            z.append(gate.astype(F32))
        conv0 = f[0:1] * z[0] + parts[0, :, cols]
        conv1 = f[0:1] * z[1] + f[1:2] * z[0] + parts[1, :, cols]
        y[0:rows, cols] = (mr[0, 0, :, cols].astype(F32) * conv0).astype(BF)
        y[rows : 2 * rows, cols] = (mr[1, 0, :, cols].astype(F32) * conv1).astype(BF)
        modal0 = parts[2, :, cols] + z[2] * r0
        modal1 = parts[3, :, cols] + z[2] * r1 + z[3] * r0
        y[2 * rows : 3 * rows, cols] = (li[0, 0, :, cols].astype(F32) * modal0).astype(BF)
        y[3 * rows : 4 * rows, cols] = (li[1, 0, :, cols].astype(F32) * modal1).astype(BF)


def project_body(engines, rows, slots_here, depth, *refs):
    ys = refs[:engines]
    mr_w, li_w = refs[engines : engines + 2]
    outs = refs[-2 - engines : -2]
    x, acc = refs[-2:]
    two = 2 * rows
    width = ys[0].shape[1]
    pw = mr_w.shape[2]
    step = pl.program_id(0)

    @pl.when(step == 0)
    def _():
        for rel in range(engines):
            for b in range(width // depth):
                x[b, 0, rel * two : (rel + 1) * two, :] = ys[rel][0:two, b * depth : (b + 1) * depth]
                x[b, 1, rel * two : (rel + 1) * two, :] = ys[rel][two : 2 * two, b * depth : (b + 1) * depth]
        acc[...] = jnp.zeros_like(acc)

    for g in range(slots_here):
        cols = slice(g * pw, (g + 1) * pw)
        acc[:, cols] += jnp.dot(x[step, 0], mr_w[g], preferred_element_type=F32) + jnp.dot(
            x[step, 1], li_w[g], preferred_element_type=F32
        )

    @pl.when(step == pl.num_programs(0) - 1)
    def _():
        for rel in range(engines):
            outs[rel][...] = acc[rel * two : (rel + 1) * two, :].astype(BF)


def sort_body(engines, chans, slots_here, slot_of, *refs):
    got = refs[:engines]
    outs = refs[-1 - chans : -1]
    tiles = refs[-1]
    pw = tiles.shape[2]
    me = lax.axis_index("engine")
    here = lax.axis_index("chan")
    per_chan = slot_of.shape[0] // chans
    for rel in range(engines):
        for g in range(slots_here):
            tiles[rel * slots_here + g] = got[rel][:, g * pw : (g + 1) * pw]
    for d in range(chans):
        there = (here + d) % chans
        for h in range(per_chan):
            slot = slot_of[there * per_chan + h]
            rel = relation_of(me, slot // slots_here, engines)
            outs[d][:, h * pw : (h + 1) * pw] = tiles[rel * slots_here + slot % slots_here]


def place_body(engines, rows, blocks, kept, layout, spread, gates, tails, near, *refs):
    msgs = refs[: len(layout)]
    if kept:
        new, tbuf, isem = refs[len(layout) :]
    else:
        new, tbuf, obuf, isem, osem = refs[len(layout) + 1 :]
    tail_len, _, width = tails.shape
    chunk = wide_chunk(width)
    lead = 2 if blocks[0] == 0 else 0

    def fetch(n):
        b = blocks[n]
        taps = sent_taps(b, tail_len)
        return pltpu.make_async_copy(tails.at[pl.ds(b * TB, taps)], tbuf.at[n, pl.ds(0, taps)], isem.at[n])

    def store(n):
        b = blocks[n]
        taps = sent_taps(b, tail_len)
        extra = lead if n == 0 else 0
        return pltpu.make_async_copy(
            obuf.at[n, pl.ds(2 - extra, taps + extra)], new.at[pl.ds(b * TB + 2 - extra, taps + extra)], osem.at[n]
        )

    for n in range(len(blocks)):
        fetch(n).start()
    if lead:
        obuf[0, 0] = gates[1]
        obuf[0, 1] = gates[0]
        edge = pltpu.make_async_copy(gates.at[4], new.at[tail_len - 1], osem.at[len(blocks)])
        edge.start()
    for n, b in enumerate(blocks):
        fetch(n).wait()
        taps = sent_taps(b, tail_len)
        top = taps * rows
        for c in range(0, width, chunk):
            cols = pl.ds(c, chunk)
            old = tbuf[n, 0:taps, :, cols].reshape(top, chunk)
            pieces = [near[b * TB * CAP : b * TB * CAP + taps * CAP, cols]]
            for msg, held in zip(msgs, layout):
                if b in held:
                    base = (b - held[0]) * TB * CAP
                    pieces.append(msg[base : base + taps * CAP, cols])
            if taps == TB:
                pieces = [jnp.concatenate(pieces, axis=0)]
            value = jnp.dot(spread[0:top, 0:top], old, preferred_element_type=F32)
            for i, piece in enumerate(pieces):
                left = TB * rows + i * TB * CAP
                value += jnp.dot(
                    spread[0:top, left : left + piece.shape[0]], piece, preferred_element_type=F32
                )
            value = value.astype(BF).reshape(taps, rows, chunk)
            if kept:
                new[n, 0:taps, :, cols] = value
            else:
                obuf[n, 2 : 2 + taps, :, cols] = value
        if not kept:
            store(n).start()
    if not kept:
        for n in range(len(blocks)):
            store(n).wait()
    if lead:
        edge.wait()


def last_body(engines, rows, blocks, spread, base, msg, _, new_tails, obuf, osem):
    tail_len, _, width = new_tails.shape
    chunk = wide_chunk(width)

    def store(n):
        b = blocks[n]
        taps = sent_taps(b, tail_len)
        return pltpu.make_async_copy(obuf.at[n, pl.ds(0, taps)], new_tails.at[pl.ds(b * TB + 2, taps)], osem.at[n])

    left = spread.shape[1] - TB * CAP
    for n, b in enumerate(blocks):
        taps = sent_taps(b, tail_len)
        top = taps * rows
        for c in range(0, width, chunk):
            cols = pl.ds(c, chunk)
            value = jnp.dot(
                spread[0:top, left : left + taps * CAP],
                msg[n * TB * CAP : n * TB * CAP + taps * CAP, cols],
                preferred_element_type=F32,
            )
            value = value + base[n, 0:taps, :, cols].reshape(top, chunk).astype(F32)
            obuf[n, 0:taps, :, cols] = value.astype(BF).reshape(taps, rows, chunk)
        store(n).start()
    for n in range(len(blocks)):
        store(n).wait()


def modal_body(engines, rows, source, slots, found, states, gates, decay, *refs):
    others = engines - 1
    msgs = refs[:others]
    new_states = refs[others]
    sbuf, z, isem, osem = refs[others + 1 :]
    modes = states.shape[1]
    me = lax.axis_index("engine")

    def fetch(r):
        return pltpu.make_async_copy(states.at[lax.rem(source[me * rows + r], rows)], sbuf.at[r], isem.at[r])

    def store(r):
        return pltpu.make_async_copy(sbuf.at[r], new_states.at[r], osem.at[r])

    def stays(r):
        return lax.div(source[me * rows + r], rows) == me

    def begin(r, carry):
        @pl.when(stays(r))
        def _():
            fetch(r).start()

        return carry

    lax.fori_loop(0, rows, begin, 0)
    z[...] = gates[2:4].astype(F32)

    def advance(r, s):
        d = decay[...]
        sbuf[r] = d * (d * s + z[0, pl.ds(r, 1), :]) + z[1, pl.ds(r, 1), :]
        store(r).start()

    for rel in range(1, engines):
        for j in range(CAP):

            @pl.when(found[rel] > j)
            def _():
                base = j * modes
                advance(slots[rel * (CAP + 1) + j], msgs[rel - 1][base : base + modes, :].astype(F32))

    def work(r, carry):
        @pl.when(stays(r))
        def _():
            fetch(r).wait()
            advance(r, sbuf[r])

        return carry

    lax.fori_loop(0, rows, work, 0)

    def finish(r, carry):
        store(r).wait()
        return carry

    lax.fori_loop(0, rows, finish, 0)


def split(total):
    cuts = [0, 2 * total // 8, 5 * total // 8, total]
    return [list(range(a, b)) for a, b in zip(cuts, cuts[1:]) if a < b]


def body(mr_qkv, li_qkv, conv_tails, modal_states, source, remaining, mr_filter, li_decay, li_residue, mr_panels,
         li_panels, panel_slot):
    engines = lax.axis_size("engine")
    chans = lax.axis_size("chan")
    rows, tail_len, width = conv_tails.shape
    modes = modal_states.shape[1]
    taps = mr_filter.shape[0]
    slots_here, _, pw = mr_panels.shape
    others = engines - 1
    chips = engines // 2
    rels = links(engines)
    far = list(range(2, engines))
    sds = jax.ShapeDtypeStruct
    dma = pltpu.SemaphoreType.DMA
    params = pltpu.CompilerParams(vmem_limit_bytes=VLIM)
    tails = jnp.transpose(conv_tails, (1, 0, 2))
    blocks = pl.cdiv(tail_len - 3, TB)
    chunks = split(blocks)
    table = pltpu.SMEM((engines * (CAP + 1),), jnp.int32)
    tally = pltpu.SMEM((engines,), jnp.int32)

    def msg_rows(i):
        return len(chunks[i]) * TB * CAP

    msgs = {}
    msgs[0] = pl.pallas_call(
        functools.partial(early_body, engines, rows, chunks[0]),
        in_specs=[ANY, ANY],
        out_specs=[VM] * len(far),
        out_shape=[sds((msg_rows(0), width), BF)] * len(far),
        scratch_shapes=[
            pltpu.SMEM(source.shape, jnp.int32),
            pltpu.VMEM((len(chunks[0]) * TB, rows, width), BF),
            pltpu.VMEM((len(far) * TB * CAP, TB * rows), BF),
            table,
            dma((len(chunks[0]),)),
            dma(()),
        ],
        compiler_params=params,
        name="early",
    )(pltpu.with_memory_space_constraint(source, pltpu.HBM), tails)
    got = {}

    def launch(i, token=None):
        arrays = list(msgs[i])
        if token is not None:
            arrays, token = lax.optimization_barrier((arrays, token))
        got[i] = [send(a, engines, *rels[rel]) for a, rel in zip(arrays, far)]
        return token

    launch(0)
    lead = pl.pallas_call(
        functools.partial(lead_body, engines, rows),
        in_specs=[SM, ANY, ANY, VM, VM, VM, ANY],
        out_specs=[VM] * (1 + others),
        out_shape=[sds((5, rows, width), F32)] + [sds((pl.cdiv(CAP * (3 + modes), 8) * 8, width), BF)] * others,
        scratch_shapes=[
            pltpu.VMEM((taps + 8, width), F32),
            pltpu.VMEM((tail_len, rows, width), BF),
            pltpu.VMEM((rows, modes, width), F32),
            table,
            dma((pl.cdiv(tail_len, TB),)),
            dma(()),
        ],
        compiler_params=params,
        name="lead",
    )(source, tails, modal_states, mr_filter, li_decay, li_residue, msgs[0][0])
    small = lead[1 : 1 + others]
    parts_got = [send(small[rel - 1], engines, *rels[rel]) for rel in range(1, engines)]

    sends = []
    for i in range(1, len(chunks)):
        sends += [(rel, chunks[i]) for rel in far]
    packed = pl.pallas_call(
        functools.partial(pack_body, engines, rows, sends),
        in_specs=[SM, ANY, VM],
        out_specs=[VM] * (3 + len(sends)) + [SM, SM],
        out_shape=[sds((blocks * TB * CAP, width), BF)]
        + [sds((CAP * sum(sent_taps(b, tail_len) for b in group), width), BF) for _, group in sends]
        + [sds((TB * rows, TB * rows + others * TB * CAP), BF), sds((5, rows, width), F32)]
        + [sds((engines * (CAP + 1),), jnp.int32), sds((engines,), jnp.int32)],
        scratch_shapes=[
            pltpu.VMEM((tail_len, rows, width), BF),
            pltpu.VMEM((others * TB * CAP, TB * rows), BF),
            table,
            dma((blocks,)),
        ],
        compiler_params=params,
        name="pack",
    )(source, tails, lead[0])
    near_msg = packed[0]
    spread, parts, arrive_slots, arrive_counts = packed[-4:]
    msgs[1] = packed[1 : 1 + len(far)]
    msgs[2] = packed[1 + len(far) : 1 + 2 * len(far)]

    y, gates = pl.pallas_call(
        functools.partial(mix_body, engines, rows),
        in_specs=[SM, SM] + [VM] * (6 + others) + [ANY] * (1 + len(far)),
        out_specs=[VM, VM],
        out_shape=[sds((4 * rows, width), BF), sds((5, rows, width), BF)],
        scratch_shapes=[pltpu.VMEM((5, rows, width), F32)],
        compiler_params=params,
        name="mix",
    )(arrive_slots, arrive_counts, parts, mr_qkv, li_qkv, mr_filter, li_decay, li_residue, *parts_got, spread, *got[0])

    near_msg, y = lax.optimization_barrier((near_msg, y))
    near_got = send(near_msg, engines, 0, 1)
    same_core = [y] + [send(y, engines, k, 0) for k in range(1, chips)]
    ys = []
    for k in range(chips):
        ys += [same_core[k], send(same_core[k], engines, 0, 1)]
    ys[1] = launch(1, ys[1])

    def place(i, arrays, layout, tails_so_far, kept=False):
        group = chunks[i]
        buffer = pltpu.VMEM((len(group), TB, rows, width), BF)
        carry = [] if kept else [gates if tails_so_far is None else tails_so_far]
        return pl.pallas_call(
            functools.partial(place_body, engines, rows, group, kept, layout),
            in_specs=[VM, VM, ANY] + [VM] * (1 + len(arrays)) + [ANY] * len(carry),
            out_specs=VM if kept else ANY,
            out_shape=sds(buffer.shape if kept else (tail_len, rows, width), BF),
            input_output_aliases={} if tails_so_far is None else {4 + len(arrays): 0},
            scratch_shapes=[buffer, dma((len(group),))]
            if kept
            else [buffer, pltpu.VMEM((len(group), TB + 2, rows, width), BF), dma((len(group),)), dma((len(group) + 1,))],
            compiler_params=params,
            name="place",
            cost_estimate=TINY,
        )(spread, gates, tails, near_got, *arrays, *carry)

    new_tails = place(0, got[0], [chunks[0]] * len(far), None)
    depth = 512
    outs = pl.pallas_call(
        functools.partial(project_body, engines, rows, slots_here, depth),
        grid=(width // depth,),
        in_specs=[pl.BlockSpec((4 * rows, width), lambda i: (0, 0))] * engines
        + [pl.BlockSpec((slots_here, depth, pw), lambda i: (0, i, 0))] * 2
        + [ANY],
        out_specs=[pl.BlockSpec((2 * rows, slots_here * pw), lambda i: (0, 0))] * engines,
        out_shape=[sds((2 * rows, slots_here * pw), BF)] * engines,
        scratch_shapes=[
            pltpu.VMEM((width // depth, 2, engines * 2 * rows, depth), BF),
            pltpu.VMEM((engines * 2 * rows, slots_here * pw), F32),
        ],
        compiler_params=params,
        name="project",
    )(*ys, mr_panels, li_panels, new_tails)

    back = [outs[0]]
    for k, f in rels[1:]:
        back.append(send(outs[2 * ((chips - k) % chips) + f], engines, k, f))
    got[1] = launch(2, got[1])

    new_states = pl.pallas_call(
        functools.partial(modal_body, engines, rows),
        in_specs=[SM, SM, SM, ANY, VM, VM] + [VM] * others,
        out_specs=ANY,
        out_shape=sds((rows, modes, width), F32),
        scratch_shapes=[
            pltpu.VMEM((rows, modes, width), F32),
            pltpu.VMEM((2, rows, width), F32),
            dma((rows,)),
            dma((rows,)),
        ],
        compiler_params=params,
        name="modal",
        cost_estimate=TINY,
    )(source, arrive_slots, arrive_counts, modal_states, gates, li_decay, *parts_got)

    back[1], new_states = lax.optimization_barrier((back[1], new_states))
    per_chan = panel_slot.shape[0] // chans
    blocks_out = pl.pallas_call(
        functools.partial(sort_body, engines, chans, slots_here),
        in_specs=[SM] + [VM] * engines + [ANY] * len(far),
        out_specs=[VM] * chans,
        out_shape=[sds((2 * rows, per_chan * pw), BF)] * chans,
        scratch_shapes=[pltpu.VMEM((engines * slots_here, 2 * rows, pw), BF)],
        compiler_params=params,
        name="sort",
        cost_estimate=TINY,
    )(panel_slot, *back, *got[1])
    total = blocks_out[0].astype(F32)
    for d in range(1, chans):
        total = total + lax.ppermute(blocks_out[d], "chan", [(c, (c + d) % chans) for c in range(chans)]).astype(F32)
    steps_ids = jnp.arange(2, dtype=jnp.int32)
    active = (remaining[None, :] > steps_ids[:, None]).astype(F32)
    total, got[2][0] = lax.optimization_barrier((total, got[2][0]))
    mixed = (total.reshape(2, rows, per_chan * pw) * active[:, :, None]).astype(BF)

    new_tails = place(1, got[1], [chunks[1]] * len(far), new_tails)
    base = place(2, got[2][:-1], [chunks[2]] * (len(far) - 1), None, True)
    buffer = pltpu.VMEM((len(chunks[2]), TB, rows, width), BF)
    new_tails = pl.pallas_call(
        functools.partial(last_body, engines, rows, chunks[2]),
        in_specs=[VM, VM, VM, ANY],
        out_specs=ANY,
        out_shape=sds((tail_len, rows, width), BF),
        input_output_aliases={3: 0},
        scratch_shapes=[buffer, dma((len(chunks[2]),))],
        compiler_params=params,
        name="last",
        cost_estimate=TINY,
    )(spread, base, got[2][-1], new_tails)
    return (mixed, jnp.transpose(new_tails, (1, 0, 2)), new_states)


def solution(mesh):
    return jax.shard_map(
        body,
        mesh=mesh,
        in_specs=(
            P(None, None, ("group", "engine"), "chan"),
            P(None, None, ("group", "engine"), "chan"),
            P(("group", "engine"), None, "chan"),
            P(("group", "engine"), None, "chan"),
            P("group"),
            P(("group", "engine")),
            P(None, "chan"),
            P(None, "chan"),
            P(None, "chan"),
            P("engine", "chan", None),
            P("engine", "chan", None),
            P(),
        ),
        out_specs=(
            P(None, ("group", "engine"), "chan"),
            P(("group", "engine"), None, "chan"),
            P(("group", "engine"), None, "chan"),
        ),
        check_vma=False,
    )
```
